32 devices in a mesh: dp: 4 (over x, core), ctx: 2 (over y), tensor: 4 (over z).
Axes of the slice: x: 2, y: 2, z: 4, core: 2. Of those that a mesh axis runs over, the one named last changes fastest.
Arguments:
- tokens: bfloat16 [4, 1024, 768], P('dp', 'ctx'), may hold values from -24 to 24
- lengths: int32 [4], P('dp'), may hold values from 128 to 1024, as said below
- cotangent: bfloat16 [4, 1024, 768], P('dp', 'ctx'), may hold values from -6 to 6
- qkv_weight: bfloat16 [3, 768, 768], P(None, 'dp', 'tensor'), may hold values from -0.21875 to 0.21875
- query_bias: float32 [768], P('tensor'), may hold values from -3 to 3
- value_bias: float32 [768], P('tensor'), may hold values from -0.18 to 0.18
- proj_weight: bfloat16 [768, 768], P('tensor', 'dp'), may hold values from -6 to 6
- proj_bias: float32 [768], replicated, may hold values from -2 to 2
- first_gain: float32 [768], replicated, may hold values from 0.1 to 1.9
- first_shift: float32 [768], replicated, may hold values from -2 to 2
- up_weight: bfloat16 [768, 3072], P('dp', 'tensor'), may hold values from -0.21875 to 0.21875
- up_bias: float32 [3072], P('tensor'), may hold values from -2 to 2
- down_weight: bfloat16 [3072, 768], P('tensor', 'dp'), may hold values from -0.109375 to 0.109375
- down_bias: float32 [768], replicated, may hold values from -2 to 2
- second_gain: float32 [768], replicated, may hold values from 0.1 to 1.9
- second_shift: float32 [768], replicated, may hold values from -2 to 2
Outputs:
- output: bfloat16 [4, 1024, 768], P('dp', 'ctx')
- grad_tokens: float32 [4, 1024, 768], P('dp', 'ctx')
- grad_qkv: float32 [3, 768, 768], P(None, 'dp', 'tensor')
- grad_query_bias: float32 [768], P('tensor')
- grad_value_bias: float32 [768], P('tensor')
- grad_proj: float32 [768, 768], P('tensor', 'dp')
- grad_proj_bias: float32 [768], replicated
- grad_first_gain: float32 [768], replicated
- grad_first_shift: float32 [768], replicated
- grad_up: float32 [768, 3072], P('dp', 'tensor')
- grad_up_bias: float32 [3072], P('tensor')
- grad_down: float32 [3072, 768], P('tensor', 'dp')
- grad_down_bias: float32 [768], replicated
- grad_second_gain: float32 [768], replicated
- grad_second_shift: float32 [768], replicated
The draws below stay inside these ranges and needn't reach their ends.
Inputs may be any that keep to these rules, and one draw needn't show every extreme that they name: `lengths`: positions at or beyond a sequence's length are padding; they are still computed, but no position attends to them.
All inputs are finite; a program needn't handle non-finite values.
Results may differ from the reference program's by a relative error of at most 0.013.
The reference program's roundings to bfloat16 on the way count: a program that leaves them out, or rounds other values in their place, can miss the bound.
Values may be sent and summed in bfloat16 or wider, within the bound.
A program may use at most 128 MiB of HBM per device.

```python
import math
import jax
import jax.numpy as jnp
from jax import lax

D = 768
H = 12
HD = 64
FF = 3072
SEQS = 4
LEN = 1024


def draw_tokens(key, part):
    base = jax.random.normal(key, (SEQS, LEN, D), jnp.float32)
    return jnp.clip(base, -6.0, 6.0).astype(jnp.bfloat16)


def draw_lengths(key, part):
    first_key, second_key = jax.random.split(jax.random.fold_in(key, 7))
    drawn = jax.random.randint(first_key, (SEQS,), LEN // 8, LEN + 1, dtype=jnp.int32)
    chosen = jax.random.randint(second_key, (), 0, SEQS, dtype=jnp.int32)
    drawn = drawn.at[chosen].set(LEN)
    drawn = drawn.at[(chosen + 1) % SEQS].set(LEN // 8)
    return drawn.astype(jnp.int32)


def block_scale(own_key, dims, cuts, low, high):
    factor_of = 1.0
    for position, shards_of in cuts:
        draws = jax.random.uniform(jax.random.fold_in(jax.random.fold_in(own_key, 6), position), (shards_of,), jnp.float32, low / len(cuts), high / len(cuts))
        factor_of = factor_of * jnp.repeat(jnp.exp(draws), dims[position] // shards_of).reshape((-1,) + (1,) * (len(dims) - 1 - position))
    return factor_of


def normal_values(rng, dims, width, most, pieces=(), held_as=jnp.bfloat16):
    gain = block_scale(rng, dims, pieces, -0.22, 0.18) if pieces else 1.0
    values = jax.random.normal(rng, dims, jnp.float32) * width * gain
    return jnp.minimum(jnp.maximum(values, -most), most).astype(held_as)


def setup_inputs(seed: int = 0) -> dict:
    streams_of = jax.random.split(jax.random.key(seed), 17)
    tokens = draw_tokens(jax.random.fold_in(streams_of[16], 71), 0)
    lengths = draw_lengths(jax.random.fold_in(streams_of[16], 71), 0)
    cotangent = normal_values(streams_of[2], (SEQS, LEN, D), 1.0, 6.0, ((0, 4), (1, 2)))
    qkv_weight = normal_values(streams_of[3], (3, D, D), D ** -0.5, 0.21875, ((1, 4), (2, 4)))
    query_bias = normal_values(streams_of[4], (D,), 0.5, 3.0, ((0, 4),), jnp.float32)
    value_bias = normal_values(streams_of[5], (D,), 0.03, 0.18, ((0, 4),), jnp.float32)
    proj_weight = normal_values(streams_of[6], (D, D), (max(1, 2 * D // LEN)) ** -0.5, 6.0, ((0, 4), (1, 4)))
    proj_bias = normal_values(streams_of[7], (D,), 0.3, 2.0, (), jnp.float32)
    first_gain = jnp.clip(1.0 + 0.18 * jax.random.normal(streams_of[8], (D,), jnp.float32), 0.1, 1.9)
    first_shift = normal_values(streams_of[9], (D,), 0.3, 2.0, (), jnp.float32)
    up_weight = normal_values(streams_of[10], (D, FF), D ** -0.5, 0.21875, ((0, 4), (1, 4)))
    up_bias = normal_values(streams_of[11], (FF,), 0.3, 2.0, ((0, 4),), jnp.float32)
    down_weight = normal_values(streams_of[12], (FF, D), FF ** -0.5, 0.109375, ((0, 4), (1, 4)))
    down_bias = normal_values(streams_of[13], (D,), 0.3, 2.0, (), jnp.float32)
    second_gain = jnp.clip(1.0 + 0.18 * jax.random.normal(streams_of[14], (D,), jnp.float32), 0.1, 1.9)
    second_shift = normal_values(streams_of[15], (D,), 0.3, 2.0, (), jnp.float32)
    return dict(tokens=tokens, lengths=lengths, cotangent=cotangent, qkv_weight=qkv_weight, query_bias=query_bias, value_bias=value_bias, proj_weight=proj_weight, proj_bias=proj_bias, first_gain=first_gain, first_shift=first_shift, up_weight=up_weight, up_bias=up_bias, down_weight=down_weight, down_bias=down_bias, second_gain=second_gain, second_shift=second_shift)


EPSILON = 1e-05
NEGATIVE = -1e+30
ROOT_HALF = 0.7071067811865476
ROOT_TWO_PI = 2.5066282746310002
HIGHEST = lax.Precision.HIGHEST

def rounded(array):
    return lax.optimization_barrier(array.astype(jnp.bfloat16))

def layer_norm(hidden_in, norm_gain, norm_shift):
    centred = hidden_in - lax.optimization_barrier(jnp.mean(hidden_in, axis=-1, keepdims=True))
    inverse = lax.rsqrt(lax.optimization_barrier(jnp.mean(centred * centred, axis=-1, keepdims=True)) + EPSILON)
    normed = centred * inverse
    return (normed * norm_gain + norm_shift, normed, inverse)

def norm_back(upstream, normed, inverse, norm_gain):
    scaled = upstream * norm_gain
    return inverse * (scaled - lax.optimization_barrier(jnp.mean(scaled, axis=-1, keepdims=True)) - normed * lax.optimization_barrier(jnp.mean(scaled * normed, axis=-1, keepdims=True)))

def gelu_value(pre_act):
    return 0.5 * pre_act * (1.0 + jax.scipy.special.erf(pre_act * ROOT_HALF))

def gelu_slope(pre_act):
    return 0.5 * (1.0 + jax.scipy.special.erf(pre_act * ROOT_HALF)) + pre_act * jnp.exp(-0.5 * pre_act * pre_act) / ROOT_TWO_PI

def attend_forward(queries, key_rows, value_rows, key_valid):
    block_rows = math.gcd(LEN, 512)
    block_count = LEN // block_rows
    score_scale = 1.0 / math.sqrt(HD)
    key_float = key_rows.astype(jnp.float32)
    value_float = value_rows.astype(jnp.float32)
    key_mask = key_valid[None, None, :]

    def one_block(query_block):
        scores = jnp.einsum('qhe,khe->hqk', query_block, key_float, precision=HIGHEST) * score_scale
        scores = jnp.where(key_mask, scores, NEGATIVE)
        row_max = lax.optimization_barrier(jnp.max(scores, axis=-1))
        weights_now = jnp.where(key_mask, jnp.exp(scores - row_max[..., None]), 0.0)
        row_total = lax.optimization_barrier(jnp.sum(weights_now, axis=-1))
        weights_low = rounded(weights_now).astype(jnp.float32)
        mixed = jnp.einsum('hqk,khe->qhe', weights_low, value_float, precision=HIGHEST)
        return (mixed / row_total.T[..., None], row_max + jnp.log(row_total))
    query_blocks = queries.astype(jnp.float32).reshape(block_count, block_rows, H, HD)
    attended, totals = lax.map(one_block, query_blocks)
    log_total = totals.transpose(1, 0, 2).reshape(H, LEN)
    return (attended.reshape(LEN, H, HD), log_total)

def attend_backward(queries, key_rows, value_rows, key_valid, d_heads, attended, log_total):
    block_rows = math.gcd(LEN, 512)
    block_count = LEN // block_rows
    score_scale = 1.0 / math.sqrt(HD)
    key_float = key_rows.astype(jnp.float32)
    value_float = value_rows.astype(jnp.float32)
    key_mask = key_valid[None, None, :]
    head_float = d_heads.astype(jnp.float32)
    row_delta = lax.optimization_barrier(jnp.sum(head_float * attended, axis=-1))

    def one_block(running, block_item):
        key_total, value_total = running
        query_block, dhead_block, delta_block, total_block = block_item
        scores = jnp.einsum('qhe,khe->hqk', query_block, key_float, precision=HIGHEST) * score_scale
        scores = jnp.where(key_mask, scores, NEGATIVE)
        probabilities = jnp.where(key_mask, jnp.exp(scores - total_block[..., None]), 0.0)
        probs_low = rounded(probabilities).astype(jnp.float32)
        value_total = value_total + jnp.einsum('hqk,qhe->khe', probs_low, dhead_block, precision=HIGHEST)
        d_probs = jnp.einsum('qhe,khe->hqk', dhead_block, value_float, precision=HIGHEST)
        d_scores = rounded(probabilities * (d_probs - delta_block.T[..., None])).astype(jnp.float32)
        d_query = jnp.einsum('hqk,khe->qhe', d_scores, key_float, precision=HIGHEST) * score_scale
        key_total = key_total + jnp.einsum('hqk,qhe->khe', d_scores, query_block, precision=HIGHEST) * score_scale
        return ((key_total, value_total), d_query)
    block_items = (queries.astype(jnp.float32).reshape(block_count, block_rows, H, HD), head_float.reshape(block_count, block_rows, H, HD), row_delta.reshape(block_count, block_rows, H), log_total.reshape(H, block_count, block_rows).transpose(1, 0, 2))
    zero_rows = jnp.zeros((LEN, H, HD), jnp.float32)
    (key_total, value_total), d_query = lax.scan(one_block, (zero_rows, zero_rows), block_items)
    return (d_query.reshape(LEN, H, HD), key_total, value_total)

def sequence_pass(seq_tokens, seq_length, seq_cot, qkv_weight, query_bias, value_bias, proj_weight, proj_bias, first_gain, first_shift, up_weight, up_bias, down_weight, down_bias, second_gain, second_shift):
    tok_float = seq_tokens.astype(jnp.float32)
    projected = jnp.einsum('td,ide->ite', tok_float, qkv_weight.astype(jnp.float32), precision=HIGHEST)
    queries = rounded(projected[0] + query_bias).reshape(LEN, H, HD)
    key_rows = rounded(projected[1]).reshape(LEN, H, HD)
    value_rows = rounded(projected[2] + value_bias).reshape(LEN, H, HD)
    key_valid = jnp.arange(LEN, dtype=jnp.int32) < seq_length
    attended, log_total = attend_forward(queries, key_rows, value_rows, key_valid)
    attended_low = rounded(attended.reshape(LEN, D))
    first_sum = tok_float + jnp.dot(attended_low, proj_weight, preferred_element_type=jnp.float32) + proj_bias
    first_out, first_normed, first_inverse = layer_norm(first_sum, first_gain, first_shift)
    first_low = rounded(first_out)
    pre_act = jnp.dot(first_low, up_weight, preferred_element_type=jnp.float32) + up_bias
    hidden = rounded(gelu_value(pre_act))
    second_sum = first_out + jnp.dot(hidden, down_weight, preferred_element_type=jnp.float32) + down_bias
    result, second_normed, second_inverse = layer_norm(second_sum, second_gain, second_shift)
    output = result.astype(jnp.bfloat16)
    upstream = seq_cot.astype(jnp.float32)
    grad_second_shift = lax.optimization_barrier(jnp.sum(upstream, axis=0))
    grad_second_gain = lax.optimization_barrier(jnp.sum(upstream * second_normed, axis=0))
    d_second = norm_back(upstream, second_normed, second_inverse, second_gain)
    grad_down_bias = lax.optimization_barrier(jnp.sum(d_second, axis=0))
    d_second_low = rounded(d_second)
    grad_down = jnp.dot(hidden.T, d_second_low, preferred_element_type=jnp.float32)
    d_pre = jnp.dot(d_second_low, down_weight.T, preferred_element_type=jnp.float32) * gelu_slope(pre_act)
    grad_up_bias = lax.optimization_barrier(jnp.sum(d_pre, axis=0))
    d_pre_low = rounded(d_pre)
    grad_up = jnp.dot(first_low.T, d_pre_low, preferred_element_type=jnp.float32)
    d_first = jnp.dot(d_pre_low, up_weight.T, preferred_element_type=jnp.float32) + d_second
    grad_first_shift = lax.optimization_barrier(jnp.sum(d_first, axis=0))
    grad_first_gain = lax.optimization_barrier(jnp.sum(d_first * first_normed, axis=0))
    d_attn = norm_back(d_first, first_normed, first_inverse, first_gain)
    grad_proj_bias = lax.optimization_barrier(jnp.sum(d_attn, axis=0))
    d_attn_low = rounded(d_attn)
    grad_proj = jnp.dot(attended_low.T, d_attn_low, preferred_element_type=jnp.float32)
    d_heads = rounded(jnp.dot(d_attn_low, proj_weight.T, preferred_element_type=jnp.float32)).reshape(LEN, H, HD)
    d_queries, d_keys, d_values = attend_backward(queries, key_rows, value_rows, key_valid, d_heads, attended, log_total)
    grad_query_bias = lax.optimization_barrier(jnp.sum(d_queries.reshape(LEN, D), axis=0))
    grad_value_bias = lax.optimization_barrier(jnp.sum(d_values.reshape(LEN, D), axis=0))
    d_stack = jnp.stack([rounded(d_queries.reshape(LEN, D)), rounded(d_keys.reshape(LEN, D)), rounded(d_values.reshape(LEN, D))]).astype(jnp.float32)
    grad_qkv = jnp.einsum('td,ite->ide', tok_float, d_stack, precision=HIGHEST)
    grad_tokens = d_attn + jnp.einsum('ite,ide->td', d_stack, qkv_weight.astype(jnp.float32), precision=HIGHEST)
    grads = (grad_qkv, grad_query_bias, grad_value_bias, grad_proj, grad_proj_bias, grad_first_gain, grad_first_shift, grad_up, grad_up_bias, grad_down, grad_down_bias, grad_second_gain, grad_second_shift)
    return ((output, grad_tokens), grads)

def reference(tokens, lengths, cotangent, qkv_weight, query_bias, value_bias, proj_weight, proj_bias, first_gain, first_shift, up_weight, up_bias, down_weight, down_bias, second_gain, second_shift):
    params = (qkv_weight, query_bias, value_bias, proj_weight, proj_bias, first_gain, first_shift, up_weight, up_bias, down_weight, down_bias, second_gain, second_shift)

    def per_sequence(totals, seq_items):
        seq_tokens, seq_length, seq_cot = seq_items
        outputs, grads = sequence_pass(seq_tokens, seq_length, seq_cot, *params)
        totals = jax.tree.map(lambda total_part, new_part: total_part + new_part, totals, grads)
        return (totals, outputs)
    zero_grads = (jnp.zeros((3, D, D), jnp.float32), jnp.zeros((D,), jnp.float32), jnp.zeros((D,), jnp.float32), jnp.zeros((D, D), jnp.float32), jnp.zeros((D,), jnp.float32), jnp.zeros((D,), jnp.float32), jnp.zeros((D,), jnp.float32), jnp.zeros((D, FF), jnp.float32), jnp.zeros((FF,), jnp.float32), jnp.zeros((FF, D), jnp.float32), jnp.zeros((D,), jnp.float32), jnp.zeros((D,), jnp.float32), jnp.zeros((D,), jnp.float32))
    totals, outputs = lax.scan(per_sequence, zero_grads, (tokens, lengths, cotangent))
    output, grad_tokens = outputs
    return (output, grad_tokens, totals[0], totals[1], totals[2], totals[3], totals[4], totals[5], totals[6], totals[7], totals[8], totals[9], totals[10], totals[11], totals[12])
```

```python
import functools
import math

import jax
import jax.numpy as jnp
from jax import lax
from jax.experimental import pallas as pl
from jax.experimental.pallas import tpu as pltpu
from jax.sharding import PartitionSpec as P

HD = 64


EPSILON = 1e-05
NEGATIVE = -1e30
ROOT_HALF = 0.7071067811865476
ROOT_TWO_PI = 2.5066282746310002
MESH = pl.DeviceIdType.MESH
BF16 = jnp.bfloat16
F32 = jnp.float32
VMEM_SPEC = pl.BlockSpec(memory_space=pltpu.VMEM)
DMA = pltpu.SemaphoreType.DMA


def layer_norm(hidden_in, norm_gain, norm_shift):
    centred = hidden_in - jnp.mean(hidden_in, axis=-1, keepdims=True)
    inverse = lax.rsqrt(jnp.mean(centred * centred, axis=-1, keepdims=True) + EPSILON)
    normed = centred * inverse
    return (normed * norm_gain + norm_shift, normed, inverse)


def norm_back(upstream, normed, inverse, norm_gain):
    scaled = upstream * norm_gain
    return inverse * (
        scaled
        - jnp.mean(scaled, axis=-1, keepdims=True)
        - normed * jnp.mean(scaled * normed, axis=-1, keepdims=True)
    )


def gelu_value(pre_act):
    return 0.5 * pre_act * (1.0 + jax.scipy.special.erf(pre_act * ROOT_HALF))


def gelu_slope(pre_act):
    return (
        0.5 * (1.0 + jax.scipy.special.erf(pre_act * ROOT_HALF))
        + pre_act * jnp.exp(-0.5 * pre_act * pre_act) / ROOT_TWO_PI
    )


def peers_of(axis, size):
    me = lax.axis_index(axis)
    found = []
    for step in range(1, size):
        other = lax.rem(me + step, size)
        found.append((other, {axis: other}))
    return found


def grid_peers(sizes):
    count = sizes["dp"] * sizes["ctx"]
    me = lax.axis_index("dp") * sizes["ctx"] + lax.axis_index("ctx")
    found = []
    for step in range(1, count):
        other = lax.rem(me + step, count)
        found.append((other, {"dp": lax.div(other, sizes["ctx"]), "ctx": lax.rem(other, sizes["ctx"])}))
    return me, found


def greet(groups):
    barrier = pltpu.get_barrier_semaphore()
    total = 0
    for group in groups:
        for _, where in group:
            pl.semaphore_signal(barrier, inc=1, device_id=where, device_id_type=MESH)
            total += 1
    pl.semaphore_wait(barrier, total)


def send_all(pairs, peers, send_sem, recv_sem):
    copies = []
    for step, (other, where) in enumerate(peers):
        source, target = pairs(other)
        copies.append(
            pltpu.make_async_remote_copy(
                src_ref=source,
                dst_ref=target,
                send_sem=send_sem.at[step],
                recv_sem=recv_sem.at[step],
                device_id=where,
                device_id_type=MESH,
            )
        )
        copies[-1].start()
    return copies


def wait_all(copies):
    for copy in copies:
        copy.wait()


def slot_sum(slots, count):
    total = slots[0].astype(F32)
    for index in range(1, count):
        total = total + slots[index].astype(F32)
    return total


def sems(count):
    return [DMA((count,)), DMA((count,))]


def call(kernel, outs, scratch, collective_id, args, name, spec=None):
    return pl.pallas_call(
        kernel,
        out_shape=outs,
        in_specs=[VMEM_SPEC] * len(args),
        out_specs=[VMEM_SPEC] * len(outs),
        scratch_shapes=scratch,
        compiler_params=pltpu.CompilerParams(
            collective_id=collective_id, has_side_effects=True, vmem_limit_bytes=56 * 2**20
        ),
        name=name,
    )(*args)


def shaped(shape, dtype):
    return jax.ShapeDtypeStruct(shape, dtype)


def pair_roles(size):
    me = lax.axis_index("dp")
    partner = me + 1 - 2 * lax.rem(me, 2)
    far = [(lax.rem(me + 2 * step, size), lax.rem(me + size - 2 * step, size)) for step in range(1, size // 2)]
    return me, partner, far


def pair_group(size):
    me, partner, far = pair_roles(size)
    return [(partner, {"dp": partner})] + [(to, {"dp": to}) for to, _ in far]


def remote(source, target, send, recv, where):
    return pltpu.make_async_remote_copy(
        src_ref=source, dst_ref=target, send_sem=send, recv_sem=recv, device_id=where, device_id_type=MESH
    )


def pair_sems(size):
    return sems(1) + sems(max(1, size // 2 - 1)) * 2


def gather_start(size, own_ref, place, sem):
    me, partner, far = pair_roles(size)
    near = remote(own_ref, place(me), sem[0].at[0], sem[1].at[0], {"dp": partner})
    wide = [
        remote(own_ref, place(me), sem[2].at[step], sem[3].at[step], {"dp": to})
        for step, (to, _) in enumerate(far)
    ]
    for copy in wide + [near]:
        copy.start()
    return near, wide


def gather_pass(size, copies, place, sem):
    me, partner, far = pair_roles(size)
    passed = []
    for step, (_, origin) in enumerate(far):
        copies[1][step].wait()
        passed.append(
            remote(place(origin), place(origin), sem[4].at[step], sem[5].at[step], {"dp": partner})
        )
        passed[-1].start()
    return [copies[0]] + passed


LAG = 4
CHUNK = 32


def line_roles(size):
    me = lax.axis_index("tensor")
    lower, upper = lax.rem(me + size - 1, size), lax.rem(me + 1, size)
    return [(me, lower, upper), (size - 1 - me, upper, lower)]


def greet_line(size, groups):
    me = lax.axis_index("tensor")
    barrier = pltpu.get_barrier_semaphore()

    @pl.when(me > 0)
    def _():
        pl.semaphore_signal(barrier, inc=1, device_id={"tensor": me - 1}, device_id_type=MESH)

    @pl.when(me < size - 1)
    def _():
        pl.semaphore_signal(barrier, inc=1, device_id={"tensor": me + 1}, device_id_type=MESH)

    total = 0
    for group in groups:
        for _, where in group:
            pl.semaphore_signal(barrier, inc=1, device_id=where, device_id_type=MESH)
            total += 1

    beside = jnp.where(me > 0, 1, 0) + jnp.where(me < size - 1, 1, 0)
    pl.semaphore_wait(barrier, total + beside)


def both(*conditions):
    return functools.reduce(jnp.logical_and, conditions)


def line_start(size, part, slots, sem):
    count = part.shape[1]
    for flow, (place, toward, _) in enumerate(line_roles(size)):

        @pl.when(place == size - 1)
        def _(flow=flow, toward=toward):
            @pl.loop(0, count)
            def _(k):
                remote(
                    part.at[flow, k], slots.at[flow, k], sem[0].at[flow, k], sem[1].at[flow, k], {"tensor": toward}
                ).start()


def line_start_block(size, part, slots, sem, flow, begin, count):
    me = lax.axis_index("tensor")
    lower, upper = lax.rem(me + size - 1, size), lax.rem(me + 1, size)
    place = jnp.where(flow == 0, me, size - 1 - me)
    toward = jnp.where(flow == 0, lower, upper)

    @pl.when(place == size - 1)
    def _():
        @pl.loop(0, count)
        def _(step):
            k = begin + step
            remote(
                part.at[flow, k], slots.at[flow, k], sem[0].at[flow, k], sem[1].at[flow, k], {"tensor": toward}
            ).start()


def line_run(size, part, slots, sums, full, sem, finish, between=(), work=None):
    count = part.shape[1]
    roles = line_roles(size)

    def reduce_copy(flow, k, source):
        return remote(
            source.at[flow, k], slots.at[flow, k], sem[0].at[flow, k], sem[1].at[flow, k], {"tensor": roles[flow][1]}
        )

    def spread_copy(flow, k):
        return remote(
            full.at[flow, k], full.at[flow, k], sem[2].at[flow, k], sem[3].at[flow, k], {"tensor": roles[flow][2]}
        )

    def one_step(step):
        if work is not None:
            work(step)

        for flow, (place, _, _) in enumerate(roles):
            k = step - LAG * (size - 1 - place)
            inside = both(k >= 0, k < count)

            @pl.when(both(inside, place > 0, place < size - 1))
            def _(flow=flow, k=k):
                reduce_copy(flow, k, sums).wait_recv()
                sums[flow, k] = (slots[flow, k].astype(F32) + part[flow, k].astype(F32)).astype(BF16)
                reduce_copy(flow, k, sums).start()

            @pl.when(both(inside, place == 0))
            def _(flow=flow, k=k):
                reduce_copy(flow, k, sums).wait_recv()
                full[flow, k] = finish(flow, k, slots[flow, k].astype(F32) + part[flow, k].astype(F32))
                spread_copy(flow, k).start()

        for flow, (place, _, _) in enumerate(roles):
            k = step - LAG * (size - 1) - LAG * place
            inside = both(k >= 0, k < count, place > 0)

            @pl.when(inside)
            def _(flow=flow, k=k):
                spread_copy(flow, k).wait_recv()

            @pl.when(both(inside, place < size - 1))
            def _(flow=flow, k=k):
                spread_copy(flow, k).start()

    begun, last = 0, count + 2 * LAG * (size - 1)
    for stop, action in tuple(between) + ((last, None),):
        stop = min(stop, last)
        pl.loop(begun, stop)(one_step)
        begun = stop
        if action is not None:
            action()

    for flow, (place, _, _) in enumerate(roles):

        @pl.when(place > 0)
        def _(flow=flow):
            @pl.loop(0, count)
            def _(k):
                reduce_copy(flow, k, sums).wait_send()

        @pl.when(place < size - 1)
        def _(flow=flow):
            @pl.loop(0, count)
            def _(k):
                spread_copy(flow, k).wait_send()


def spread_start(size, mine, full, sem):
    for flow, (place, _, away) in enumerate(line_roles(size)):

        @pl.when(place == 0)
        def _(flow=flow, away=away):
            @pl.loop(0, mine.shape[0])
            def _(k):
                remote(
                    mine.at[k], full.at[flow, k], sem[0].at[flow, k], sem[1].at[flow, k], {"tensor": away}
                ).start()
                full[flow, k] = mine[k]


def spread_run(size, mine, full, sem):
    count = mine.shape[0]
    roles = line_roles(size)

    def pass_on(flow, k):
        return remote(
            full.at[flow, k], full.at[flow, k], sem[0].at[flow, k], sem[1].at[flow, k], {"tensor": roles[flow][2]}
        )

    @pl.loop(0, count + LAG * (size - 1))
    def _(step):
        for flow, (place, _, _) in enumerate(roles):
            k = step - LAG * place
            inside = both(k >= 0, k < count, place > 0)

            @pl.when(inside)
            def _(flow=flow, k=k):
                pass_on(flow, k).wait_recv()

            @pl.when(both(inside, place < size - 1))
            def _(flow=flow, k=k):
                pass_on(flow, k).start()

    for flow, (place, _, _) in enumerate(roles):

        @pl.when(place < size - 1)
        def _(flow=flow):
            @pl.loop(0, count)
            def _(k):
                pass_on(flow, k).wait_send()


def line_sems(count, kinds):
    return [DMA((2, count))] * kinds


def add_row(vector_ref, index, value):
    vector_ref[index : index + 1] += jnp.sum(value, axis=0, keepdims=True)


CONTRACT_LAST = (((1,), (1,)), ((), ()))
CONTRACT_FIRST = (((0,), (0,)), ((), ()))


PIECES = 4
GROUP = 4
ROW_BLOCK = 256


def matmul(left, right):
    return jnp.dot(left, right, preferred_element_type=F32)


def matmul_last(left, right):
    return lax.dot_general(left, right, CONTRACT_LAST, preferred_element_type=F32)


def matmul_first(left, right):
    return lax.dot_general(left, right, CONTRACT_FIRST, preferred_element_type=F32)


def part_rows(index, count):
    return pl.ds(pl.multiple_of(index * count, count), count)


def block_of(step, group):
    return lax.rem(step, 2), lax.div(step, 2) * group


def gather_kernel(sizes, tokens, qkv, proj, wide_tokens, wide_qkv, wide_proj, *sem):
    data, blocks, ranks = sizes["dp"], sizes["ctx"], sizes["tensor"]
    me, rank = lax.axis_index("ctx"), lax.axis_index("tensor")
    mate = rank + 1 - 2 * lax.rem(rank, 2)
    peers = peers_of("ctx", blocks)
    piece = qkv.shape[1]
    rows = tokens.shape[0] // 2 // PIECES

    def span(parity, index):
        return pl.ds(pl.multiple_of((parity * PIECES + index) * rows, rows), rows)

    own_half = lax.rem(rank, 2)
    greet([peers, [(mate, {"tensor": mate})], pair_group(data)])
    across = []
    for index in range(PIECES):
        for step, (_, where) in enumerate(peers):
            here = span(own_half, index)
            across.append(
                remote(tokens.at[here], wide_tokens.at[me, here], sem[0].at[step, index], sem[1].at[step, index], where)
            )
            across[-1].start()
    place_qkv = lambda index: wide_qkv.at[:, part_rows(index, piece)]
    place_proj = lambda index: wide_proj.at[index]
    copies = gather_start(data, qkv, place_qkv, sem[4:10])
    projs = gather_start(data, proj, place_proj, sem[10:16])
    mine = lax.axis_index("dp")
    wide_qkv[:, part_rows(mine, piece)] = qkv[...]
    wide_proj[mine] = proj[...]
    wide_tokens[me] = tokens[...]
    passed = []
    for index in range(PIECES):
        for step in range(len(peers)):
            origin = lax.rem(me + blocks - step - 1, blocks)
            across[index * len(peers) + step].wait_recv()
            here = span(own_half, index)
            place = wide_tokens.at[origin, here]
            passed.append(
                remote(place, place, sem[2].at[step, index], sem[3].at[step, index], {"tensor": mate})
            )
            passed[-1].start()
    passing = gather_pass(data, copies, place_qkv, sem[4:10])
    passing += gather_pass(data, projs, place_proj, sem[10:16])
    for copy in across:
        copy.wait_send()
    wait_all(passed)
    wait_all(passing)


def forward_kernel(
    sizes, score_scale, length_ref, tokens, wide_tokens, wide_qkv, wide_proj, fixed,
    q_ref, k_ref, v_ref, out_ref, low_ref, log_ref, part_ref, proj_ref, flat_ref
):
    length = length_ref[0]
    rows, width = q_ref.shape
    keys = k_ref.shape[0]
    block = math.gcd(rows, ROW_BLOCK)
    column = wide_proj.shape[2]
    for index in range(sizes["dp"]):
        proj_ref[:, index * column : (index + 1) * column] = wide_proj[index]
    for slot, index in enumerate((1, 2, 0)):
        flat_ref[:, slot * width : (slot + 1) * width] = wide_qkv[index]

    @pl.loop(0, keys // block)
    def _(step):
        here = part_rows(step, block)
        found = wide_tokens[here]
        k_ref[here] = matmul(found, wide_qkv[1]).astype(BF16)
        v_ref[here] = (matmul(found, wide_qkv[2]) + fixed[8:9, :width]).astype(BF16)

    hidden_keys = lax.broadcasted_iota(jnp.int32, (block, keys), 1) >= length

    @pl.loop(0, rows // block)
    def _(step):
        here = part_rows(step, block)
        q_ref[here] = (matmul(tokens[here], wide_qkv[0]) + fixed[7:8, :width]).astype(BF16)
        for head in range(width // HD):
            lanes = slice(head * HD, (head + 1) * HD)
            scores = matmul_last(q_ref[here, lanes], k_ref[:, lanes]) * score_scale
            scores = jnp.where(hidden_keys, NEGATIVE, scores)
            top = jnp.max(scores, axis=-1, keepdims=True)
            weights = jnp.exp(scores - top)
            total = jnp.sum(weights, axis=-1, keepdims=True)
            attended = matmul(weights.astype(BF16), v_ref[:, lanes]) / total
            out_ref[here, lanes] = attended
            low_ref[here, lanes] = attended.astype(BF16)
            log_ref[here, head : head + 1] = top + jnp.log(total)
        part_ref[here] = matmul(low_ref[here], proj_ref[...]).astype(BF16)


def near_start(size, grads, chip, sem):
    _, partner, _ = pair_roles(size)
    piece = chip.shape[1]
    copies = [
        remote(
            grads.at[part_rows(2 * index + lax.rem(partner, 2), piece)],
            chip.at[index],
            sem[0].at[index],
            sem[1].at[index],
            {"dp": partner},
        )
        for index in range(size // 2)
    ]
    for copy in copies:
        copy.start()
    return copies


def far_start(size, copies, grads, chip, merged, slots, sem):
    me, _, far = pair_roles(size)
    piece = chip.shape[1]
    wait_all(copies)
    for index in range(size // 2):
        own = grads[part_rows(2 * index + lax.rem(me, 2), piece)]
        merged[index] = (own.astype(F32) + chip[index].astype(F32)).astype(BF16)
    moving = [
        remote(
            merged.at[lax.div(to, 2)], slots.at[lax.div(me, 2)], sem[2].at[step], sem[3].at[step], {"dp": to}
        )
        for step, (to, _) in enumerate(far)
    ]
    for copy in moving:
        copy.start()
    slots[lax.div(me, 2)] = merged[lax.div(me, 2)]
    return moving


def blocks_start(sizes, value, blocks, sem):
    me = lax.axis_index("ctx")
    blocks[me] = value
    return send_all(
        lambda other: (blocks.at[me], blocks.at[me]), peers_of("ctx", sizes["ctx"]), sem[0], sem[1]
    )


def middle_kernel(
    sizes, part, tokens, cotangent, fixed, up, down,
    attn_low, attn_ref, output_ref, vector_ref, block_up, block_down,
    wide_up, wide_down, low, normed_ref, inverse_ref, out_ref, pre, hidden,
    part_two, back_ref, second_low, d_pre, part_three, grads_up, grads_down,
    slots, sums, slots_two, sums_two, slots_three, sums_three,
    chip_a, chip_b, merged_a, merged_b, far_a, far_b, *sem
):
    size, data = sizes["tensor"], sizes["dp"]
    mine = lax.axis_index("dp")
    piece = up.shape[0]
    chunks, chunk, model = part.shape[1:]
    group = math.gcd(chunks, GROUP)
    count = group * chunk
    steps = 2 * chunks // group
    line_one, line_two, line_three = sem[0:4], sem[4:8], sem[8:12]
    sem_up, sem_down = sem[12:18], sem[18:24]
    sem_a, sem_b = sem[24:28], sem[28:32]
    greet_line(size, [pair_group(data)])
    line_start(size, part, slots, line_one)
    place_up = lambda index: wide_up.at[part_rows(index, piece)]
    place_down = lambda index: wide_down.at[part_rows(index, piece)]
    ups = gather_start(data, up, place_up, sem_up)
    downs = gather_start(data, down, place_down, sem_down)
    wide_up[part_rows(mine, piece)] = up[...]
    wide_down[part_rows(mine, piece)] = down[...]
    vector_ref[...] = jnp.zeros_like(vector_ref)

    def first_finish(flow, k, total):
        first_sum = tokens[flow, k].astype(F32) + total + fixed[0:1, :model]
        first_out, normed, inverse = layer_norm(first_sum, fixed[1:2, :model], fixed[2:3, :model])
        out_ref[k] = first_out
        normed_ref[k] = normed
        inverse_ref[k] = inverse
        return first_out.astype(BF16)

    passed = []

    def hand_over():
        passed.extend(gather_pass(data, ups, place_up, sem_up))
        passed.extend(gather_pass(data, downs, place_down, sem_down))

    line_run(size, part, slots, sums, low, line_one, first_finish, [(LAG * size, hand_over)])
    wait_all(passed)

    @pl.loop(0, steps)
    def _(step):
        flow, begin = block_of(step, group)
        here = pl.ds(pl.multiple_of(step * count, count), count)
        found = low[flow, pl.ds(begin, group)].reshape(count, model)
        value = matmul(found, wide_up[...]) + fixed[6:7, : pre.shape[1]]
        pre[here] = value
        hidden[here] = gelu_value(value).astype(BF16)
        result = matmul_last(hidden[here], wide_down[...]).astype(BF16)
        part_two[flow, pl.ds(begin, group)] = result.reshape(group, chunk, model)
        line_start_block(size, part_two, slots_two, line_two, flow, begin, group)

    def second_finish(flow, k, total):
        second_sum = out_ref[k] + total + fixed[3:4, :model]
        result, normed, inverse = layer_norm(second_sum, fixed[4:5, :model], fixed[5:6, :model])
        upstream = cotangent[flow, k].astype(F32)
        d_second = norm_back(upstream, normed, inverse, fixed[4:5, :model])
        output_ref[k] = result.astype(BF16)
        back_ref[k] = d_second
        add_row(vector_ref, 0, upstream)
        add_row(vector_ref, 1, upstream * normed)
        add_row(vector_ref, 2, d_second)
        return d_second.astype(BF16)

    def slope_work(step):
        @pl.when(step < 2 * chunks)
        def _():
            here = part_rows(step, chunk)
            pre[here] = gelu_slope(pre[here])

    line_run(size, part_two, slots_two, sums_two, second_low, line_two, second_finish, work=slope_work)

    @pl.loop(0, steps)
    def _(step):
        flow, begin = block_of(step, group)
        here = pl.ds(pl.multiple_of(step * count, count), count)
        found = second_low[flow, pl.ds(begin, group)].reshape(count, model)
        value = matmul(found, wide_down[...]) * pre[here]
        add_row(vector_ref, 6, value)
        d_pre[here] = value.astype(BF16)
        result = matmul_last(d_pre[here], wide_up[...]).astype(BF16)
        part_three[flow, pl.ds(begin, group)] = result.reshape(group, chunk, model)
        line_start_block(size, part_three, slots_three, line_three, flow, begin, group)

    def third_finish(flow, k, total):
        d_first = total + back_ref[k]
        normed = normed_ref[k]
        d_attn = norm_back(d_first, normed, inverse_ref[k], fixed[1:2, :model])
        attn_ref[k] = d_attn
        add_row(vector_ref, 3, d_first)
        add_row(vector_ref, 4, d_first * normed)
        add_row(vector_ref, 5, d_attn)
        return d_attn.astype(BF16)

    pieces = model // 128

    def grads_work(step):
        @pl.when(step < pieces)
        def _():
            columns = part_rows(step, 128)
            left = [
                second_low[block % 2, block // 2 * group : block // 2 * group + group, :, columns].reshape(count, 128)
                for block in range(steps)
            ]
            grads_down[columns] = matmul_first(jnp.concatenate(left, axis=0), hidden[...]).astype(BF16)

        @pl.when(jnp.logical_and(step >= pieces, step < 2 * pieces))
        def _():
            columns = part_rows(step - pieces, 128)
            left = [
                low[block % 2, block // 2 * group : block // 2 * group + group, :, columns].reshape(count, 128)
                for block in range(steps)
            ]
            grads_up[columns] = matmul_first(jnp.concatenate(left, axis=0), d_pre[...]).astype(BF16)

    near_a, near_b, moving_a, moving_b = [], [], [], []

    def near_down():
        near_b.extend(near_start(data, grads_down, chip_b, sem_b))

    def near_up():
        near_a.extend(near_start(data, grads_up, chip_a, sem_a))
        moving_b.extend(far_start(data, near_b, grads_down, chip_b, merged_b, far_b, sem_b))

    def far_up():
        moving_a.extend(far_start(data, near_a, grads_up, chip_a, merged_a, far_a, sem_a))

    between = [(pieces, near_down), (2 * pieces, near_up), (2 * pieces + LAG, far_up)]
    line_run(
        size, part_three, slots_three, sums_three, attn_low, line_three, third_finish, between, work=grads_work
    )
    wait_all(moving_b)
    block_down[...] = slot_sum(far_b, data // 2).astype(BF16)
    wait_all(moving_a)
    block_up[...] = slot_sum(far_a, data // 2).astype(BF16)


def backward_kernel(
    sizes, score_scale, length_ref, q_ref, k_ref, v_ref, attended_ref, low_ref, log_ref,
    proj_ref, attn_low, tokens, vectors,
    stack_ref, grads_ref, vector_ref,
    dk_ref, dv_ref, heads_ref
):
    length = length_ref[0]
    rows, width = q_ref.shape
    keys = k_ref.shape[0]
    me = lax.axis_index("ctx")
    block = math.gcd(rows, ROW_BLOCK)
    hidden_keys = lax.broadcasted_iota(jnp.int32, (block, keys), 1) >= length
    dk_ref[...] = jnp.zeros_like(dk_ref)
    dv_ref[...] = jnp.zeros_like(dv_ref)
    vector_ref[...] = vectors[...]
    stack_ref[:, 2 * width :] = jnp.zeros((keys, width), BF16)

    @pl.loop(0, rows // block)
    def _(step):
        here = part_rows(step, block)
        there = pl.ds(pl.multiple_of(me * rows + step * block, block), block)
        heads_ref[here] = matmul_last(attn_low[here], proj_ref[...]).astype(BF16)
        for head in range(width // HD):
            lanes = slice(head * HD, (head + 1) * HD)
            q, k, v, d_heads = q_ref[here, lanes], k_ref[:, lanes], v_ref[:, lanes], heads_ref[here, lanes]
            delta = jnp.sum(d_heads.astype(F32) * attended_ref[here, lanes], axis=-1, keepdims=True)
            scores = matmul_last(q, k) * score_scale
            scores = jnp.where(hidden_keys, NEGATIVE, scores)
            probs = jnp.exp(scores - log_ref[here, head : head + 1])
            d_scores = (probs * (matmul_last(d_heads, v) - delta)).astype(BF16)
            dv_ref[:, lanes] += matmul_first(probs.astype(BF16), d_heads)
            dk_ref[:, lanes] += matmul_first(d_scores, q) * score_scale
            d_query = matmul(d_scores, k) * score_scale
            vector_ref[7:8, lanes] += jnp.sum(d_query, axis=0, keepdims=True)
            stack_ref[there, 2 * width + head * HD : 2 * width + (head + 1) * HD] = d_query.astype(BF16)

    vector_ref[7:8, width : 2 * width] = jnp.sum(dv_ref[...], axis=0, keepdims=True)
    stack_ref[:, :width] = dk_ref[...].astype(BF16)
    stack_ref[:, width : 2 * width] = dv_ref[...].astype(BF16)

    @pl.loop(0, grads_ref.shape[0] // 128)
    def _(index):
        columns = part_rows(index, 128)
        grads_ref[columns, : 3 * width] = matmul_first(tokens[:, columns], stack_ref[...]).astype(BF16)
        grads_ref[columns, 3 * width :] = matmul_first(attn_low[:, columns], low_ref[...]).astype(BF16)


def last_kernel(
    sizes, stack, flat, d_attn, grads, block_a, block_b, vectors, mine,
    full, output_ref, owned, owned_a, owned_b, vector_ref,
    part, slots, sums, keys, total_ref, chip, merged, far, blocks, blocks_a, blocks_b, slots_v, grid_v, *sem
):
    size, data = sizes["tensor"], sizes["dp"]
    me, block = lax.axis_index("tensor"), lax.axis_index("ctx")
    chunks, chunk, model = part.shape[1:]
    group = math.gcd(chunks, GROUP)
    count = group * chunk
    steps = 2 * chunks // group
    wide = keys.shape[2]
    line, spread, sem_keys, sem_grads = sem[0:4], sem[4:6], sem[6:8], sem[8:12]
    sem_small, sem_grid, sem_a, sem_b, sem_last = sem[12:14], sem[14:16], sem[16:18], sem[18:20], sem[20:22]
    rows = peers_of("tensor", size)
    others = peers_of("ctx", sizes["ctx"])
    here, everyone = grid_peers(sizes)
    greet([rows, everyone])

    def span(step):
        flow, begin = step % 2, step // 2 * group
        return slice((flow * chunks + begin) * chunk, (flow * chunks + begin) * chunk + count)

    moving_keys = [
        [
            remote(
                stack.at[other, span(step), 0:wide],
                keys.at[block, span(step)],
                sem_keys[0].at[index, step],
                sem_keys[1].at[index, step],
                where,
            )
            for index, (other, where) in enumerate(others)
        ]
        for step in range(steps)
    ]
    for copies in moving_keys:
        for copy in copies:
            copy.start()
    near = near_start(data, grads, chip, sem_grads)
    spread_start(size, mine, output_ref, spread)
    small = send_all(lambda other: (vectors, slots_v.at[me]), rows, sem_small[0], sem_small[1])
    moving_a = blocks_start(sizes, block_a[...], blocks_a, sem_a)
    moving_b = blocks_start(sizes, block_b[...], blocks_b, sem_b)
    slots_v[me] = vectors[...]
    state = {}

    def send_group(step):
        flow, begin = step % 2, step // 2 * group
        there = span(step)
        keys[block, there] = stack[block, there, 0:wide]
        for copy in moving_keys[step]:
            copy.wait_recv()
        total = keys[0, there].astype(F32)
        for index in range(1, sizes["ctx"]):
            total = total + keys[index, there].astype(F32)
        total_ref[there, 0:wide] = total.astype(BF16)
        total_ref[there, wide:] = stack[block, there, wide:]
        result = matmul_last(total_ref[there], flat[...]).astype(BF16)
        part[flow, begin : begin + group] = result.reshape(group, chunk, model)
        line_start_block(size, part, slots, line, flow, begin, group)

    def go_far():
        state["far"] = far_start(data, near, grads, chip, merged, far, sem_grads)
        wait_all(small)
        own = vectors[...]
        row_ids = lax.broadcasted_iota(jnp.int32, own.shape, 0)
        grid_v[here] = jnp.where(row_ids < 6, slot_sum(slots_v, size), own)
        state["small"] = send_all(
            lambda other: (grid_v.at[here], grid_v.at[here]), everyone, sem_grid[0], sem_grid[1]
        )

    def go_across():
        wait_all(state["far"])
        value = slot_sum(far, data // 2).astype(BF16)
        state["across"] = blocks_start(sizes, value, blocks, sem_last)

    def finish(flow, k, total):
        return (total + d_attn[k]).astype(BF16)

    for step in range(2):
        send_group(step)
    between = [(1, go_far)]
    between += [(LAG + 2 * step - 3, functools.partial(send_group, step)) for step in range(2, steps)]
    between += [(max(LAG * size, LAG + 2 * steps), go_across)]
    line_run(size, part, slots, sums, full, line, finish, between)
    spread_run(size, mine, output_ref, spread)
    for copies in moving_keys:
        for copy in copies:
            copy.wait_send()
    wait_all(state["small"])
    vector_ref[...] = slot_sum(grid_v, data * sizes["ctx"])
    wait_all(moving_a)
    owned_a[...] = slot_sum(blocks_a, sizes["ctx"])
    wait_all(moving_b)
    owned_b[...] = slot_sum(blocks_b, sizes["ctx"])
    wait_all(state["across"])
    owned[...] = slot_sum(blocks, sizes["ctx"])


def unpack_kernel(
    full, output, owned, owned_a, owned_b,
    output_ref, tokens_ref, qkv_ref, proj_ref, up_ref, down_ref
):
    width = qkv_ref.shape[2]
    output_ref[...] = output[...]
    tokens_ref[...] = full[...].astype(F32)
    for index, slot in enumerate((2, 0, 1)):
        qkv_ref[index] = owned[:, slot * width : (slot + 1) * width]
    proj_ref[...] = owned[:, 3 * width :].T
    up_ref[...] = owned_a[...]
    down_ref[...] = owned_b[...]


def local_call(kernel, outs, scratch, args, name, scalars=1):
    return pl.pallas_call(
        kernel,
        out_shape=outs,
        in_specs=[pl.BlockSpec(memory_space=pltpu.SMEM)] * scalars + [VMEM_SPEC] * (len(args) - scalars),
        out_specs=[VMEM_SPEC] * len(outs),
        scratch_shapes=scratch,
        compiler_params=pltpu.CompilerParams(vmem_limit_bytes=60 * 2**20),
        name=name,
    )(*args)


def per_device(
    sizes,
    tokens,
    lengths,
    cotangent,
    qkv_weight,
    query_bias,
    value_bias,
    proj_weight,
    proj_bias,
    first_gain,
    first_shift,
    up_weight,
    up_bias,
    down_weight,
    down_bias,
    second_gain,
    second_shift,
):
    data, blocks, ranks = sizes["dp"], sizes["ctx"], sizes["tensor"]
    rows_in = tokens[0]
    row_count, model = rows_in.shape
    half = row_count // 2
    chunk = math.gcd(half, CHUNK)
    chunks = half // chunk
    piece, width = qkv_weight.shape[1:]
    up_width = up_weight.shape[1]
    keys = blocks * row_count
    score_scale = 1.0 / math.sqrt(HD)
    split = (2, chunks, chunk, model)
    flow = pltpu.VMEM(split, BF16)
    line = line_sems(chunks, 4)
    local = shaped(split[1:], F32)
    held = pltpu.VMEM(split[1:], F32)
    steps = 2 * chunks // math.gcd(chunks, GROUP)
    vector_width = max(model, up_width, 2 * width)
    fixed = jnp.zeros((16, vector_width), F32)
    row_ids = lax.broadcasted_iota(jnp.int32, fixed.shape, 0)
    for index, vector in enumerate(
        [
            proj_bias, first_gain, first_shift, down_bias, second_gain, second_shift,
            up_bias, query_bias, value_bias,
        ]
    ):
        padded = jnp.pad(vector, (0, vector_width - vector.shape[0]))
        fixed = jnp.where(row_ids == index, padded[None], fixed)

    wide_tokens, wide_qkv, wide_proj = call(
        functools.partial(gather_kernel, sizes),
        [
            shaped((blocks, row_count, model), BF16),
            shaped((3, model, width), BF16),
            shaped((data,) + proj_weight.shape, BF16),
        ],
        [DMA((blocks - 1, PIECES))] * 4 + pair_sems(data) * 2,
        0,
        (rows_in, qkv_weight, proj_weight),
        "gather_inputs",
    )
    wide_tokens = wide_tokens.reshape(keys, model)
    queries, key_rows, value_rows, attended, attended_low, log_total, attn_part, flat_proj, flat_qkv = local_call(
        functools.partial(forward_kernel, sizes, score_scale),
        [
            shaped((row_count, width), BF16),
            shaped((keys, width), BF16),
            shaped((keys, width), BF16),
            shaped((row_count, width), F32),
            shaped((row_count, width), BF16),
            shaped((row_count, width // HD), F32),
            shaped((row_count, model), BF16),
            shaped((width, model), BF16),
            shaped((model, 3 * width), BF16),
        ],
        [],
        (lengths, rows_in, wide_tokens, wide_qkv, wide_proj, fixed),
        "attention_forward",
    )

    up_shape = (model, up_width)
    pair_slots = pltpu.VMEM((data // 2, model // data, up_width), BF16)
    pair_moves = sems(data // 2) + sems(max(1, data // 2 - 1))
    attn_low, d_attn, output_part, vectors, block_up, block_down = call(
        functools.partial(middle_kernel, sizes),
        [
            shaped(split, BF16),
            local,
            shaped(split[1:], BF16),
            shaped((8, vector_width), F32),
            shaped((model // data, up_width), BF16),
            shaped((model // data, up_width), BF16),
        ],
        [
            pltpu.VMEM(up_shape, BF16),
            pltpu.VMEM(up_shape, BF16),
            flow,
            held,
            pltpu.VMEM((chunks, chunk, 1), F32),
            held,
            pltpu.VMEM((row_count, up_width), F32),
            pltpu.VMEM((row_count, up_width), BF16),
            flow,
            held,
            flow,
            pltpu.VMEM((row_count, up_width), BF16),
            flow,
            pltpu.VMEM(up_shape, BF16),
            pltpu.VMEM(up_shape, BF16),
        ]
        + [flow] * 6
        + [pair_slots] * 6
        + line * 3
        + pair_sems(data) * 2
        + pair_moves * 2,
        1,
        (
            attn_part.reshape(split),
            rows_in.reshape(split),
            cotangent[0].reshape(split),
            fixed,
            up_weight,
            down_weight.T,
        ),
        "norms_and_hidden",
    )

    stack, last_grads, vectors = local_call(
        functools.partial(backward_kernel, sizes, score_scale),
        [
            shaped((keys, 3 * width), BF16),
            shaped((model, 4 * width), BF16),
            shaped(vectors.shape, F32),
        ],
        [
            pltpu.VMEM((keys, width), F32),
            pltpu.VMEM((keys, width), F32),
            pltpu.VMEM((row_count, width), BF16),
        ],
        (
            lengths, queries, key_rows, value_rows, attended, attended_low, log_total,
            flat_proj, attn_low.reshape(row_count, model), wide_tokens, vectors,
        ),
        "attention_backward",
    )

    own_shape = (model // data, 4 * width)
    last_pair = pltpu.VMEM((data // 2,) + own_shape, BF16)
    grad_tokens, output, own_last, own_up, own_down, sums = call(
        functools.partial(last_kernel, sizes),
        [
            shaped(split, BF16),
            shaped(split, BF16),
            shaped(own_shape, F32),
            shaped((model // data, up_width), F32),
            shaped((model // data, up_width), F32),
            shaped(vectors.shape, F32),
        ],
        [flow] * 3
        + [
            pltpu.VMEM((blocks, row_count, 2 * width), BF16),
            pltpu.VMEM((row_count, 3 * width), BF16),
        ]
        + [last_pair] * 3
        + [pltpu.VMEM((blocks,) + own_shape, BF16)]
        + [pltpu.VMEM((blocks, model // data, up_width), BF16)] * 2
        + [
            pltpu.VMEM((ranks,) + vectors.shape, F32),
            pltpu.VMEM((data * blocks,) + vectors.shape, F32),
        ]
        + line
        + line_sems(chunks, 2)
        + [DMA((max(1, blocks - 1), steps))] * 2
        + pair_moves
        + sems(ranks - 1)
        + sems(data * blocks - 1)
        + sems(blocks - 1) * 3,
        2,
        (
            stack.reshape(blocks, row_count, 3 * width),
            flat_qkv,
            d_attn,
            last_grads,
            block_up,
            block_down,
            vectors,
            output_part,
        ),
        "token_grads",
    )
    output, grad_tokens, own_qkv, own_proj, own_up, own_down = local_call(
        unpack_kernel,
        [
            shaped((row_count, model), BF16),
            shaped((row_count, model), F32),
            shaped((3, model // data, width), F32),
            shaped((width, model // data), F32),
            shaped(own_up.shape, F32),
            shaped(own_down.shape, F32),
        ],
        [],
        (
            grad_tokens.reshape(row_count, model),
            output.reshape(row_count, model),
            own_last,
            own_up,
            own_down,
        ),
        "unpack",
        scalars=0,
    )
    return (
        output[None],
        grad_tokens[None],
        own_qkv,
        sums[7, :width],
        sums[7, width : 2 * width],
        own_proj,
        sums[5, :model],
        sums[4, :model],
        sums[3, :model],
        own_up,
        sums[6, :up_width],
        own_down.T,
        sums[2, :model],
        sums[1, :model],
        sums[0, :model],
    )


def solution(mesh):
    placed = (
        P("dp", "ctx", None),
        P("dp"),
        P("dp", "ctx", None),
        P(None, "dp", "tensor"),
        P("tensor"),
        P("tensor"),
        P("tensor", "dp"),
        P(),
        P(),
        P(),
        P("dp", "tensor"),
        P("tensor"),
        P("tensor", "dp"),
        P(),
        P(),
        P(),
    )
    return jax.shard_map(
        functools.partial(per_device, dict(mesh.shape)),
        mesh=mesh,
        in_specs=placed,
        out_specs=(
            P("dp", "ctx", None),
            P("dp", "ctx", None),
            P(None, "dp", "tensor"),
            P("tensor"),
            P("tensor"),
            P("tensor", "dp"),
            P(),
            P(),
            P(),
            P("dp", "tensor"),
            P("tensor"),
            P("tensor", "dp"),
            P(),
            P(),
            P(),
        ),
        check_vma=False,
    )
```

```python
import functools
import math

import jax
import jax.numpy as jnp
from jax import lax
from jax.experimental import pallas as pl
from jax.experimental.pallas import tpu as pltpu
from jax.sharding import PartitionSpec as P

HD = 64


EPSILON = 1e-05
NEGATIVE = -1e30
ROOT_HALF = 0.7071067811865476
ROOT_TWO_PI = 2.5066282746310002
MESH = pl.DeviceIdType.MESH
BF16 = jnp.bfloat16
F32 = jnp.float32
VMEM_SPEC = pl.BlockSpec(memory_space=pltpu.VMEM)
DMA = pltpu.SemaphoreType.DMA


def layer_norm(hidden_in, norm_gain, norm_shift):
    centred = hidden_in - jnp.mean(hidden_in, axis=-1, keepdims=True)
    inverse = lax.rsqrt(jnp.mean(centred * centred, axis=-1, keepdims=True) + EPSILON)
    normed = centred * inverse
    return (normed * norm_gain + norm_shift, normed, inverse)


def norm_back(upstream, normed, inverse, norm_gain):
    scaled = upstream * norm_gain
    return inverse * (
        scaled
        - jnp.mean(scaled, axis=-1, keepdims=True)
        - normed * jnp.mean(scaled * normed, axis=-1, keepdims=True)
    )


def gelu_value(pre_act):
    return 0.5 * pre_act * (1.0 + jax.scipy.special.erf(pre_act * ROOT_HALF))


def gelu_slope(pre_act):
    return (
        0.5 * (1.0 + jax.scipy.special.erf(pre_act * ROOT_HALF))
        + pre_act * jnp.exp(-0.5 * pre_act * pre_act) / ROOT_TWO_PI
    )


def peers_of(axis, size):
    me = lax.axis_index(axis)
    found = []
    for step in range(1, size):
        other = lax.rem(me + step, size)
        found.append((other, {axis: other}))
    return found


def grid_peers(sizes):
    count = sizes["dp"] * sizes["ctx"]
    me = lax.axis_index("dp") * sizes["ctx"] + lax.axis_index("ctx")
    found = []
    for step in range(1, count):
        other = lax.rem(me + step, count)
        found.append((other, {"dp": lax.div(other, sizes["ctx"]), "ctx": lax.rem(other, sizes["ctx"])}))
    return me, found


def greet(groups):
    barrier = pltpu.get_barrier_semaphore()
    total = 0
    for group in groups:
        for _, where in group:
            pl.semaphore_signal(barrier, inc=1, device_id=where, device_id_type=MESH)
            total += 1
    pl.semaphore_wait(barrier, total)


def send_all(pairs, peers, send_sem, recv_sem):
    copies = []
    for step, (other, where) in enumerate(peers):
        source, target = pairs(other)
        copies.append(
            pltpu.make_async_remote_copy(
                src_ref=source,
                dst_ref=target,
                send_sem=send_sem.at[step],
                recv_sem=recv_sem.at[step],
                device_id=where,
                device_id_type=MESH,
            )
        )
        copies[-1].start()
    return copies


def wait_all(copies):
    for copy in copies:
        copy.wait()


def slot_sum(slots, count):
    total = slots[0].astype(F32)
    for index in range(1, count):
        total = total + slots[index].astype(F32)
    return total


def sems(count):
    return [DMA((count,)), DMA((count,))]


def call(kernel, outs, scratch, collective_id, args, name, scalars=0):
    return pl.pallas_call(
        kernel,
        out_shape=outs,
        in_specs=[pl.BlockSpec(memory_space=pltpu.SMEM)] * scalars + [VMEM_SPEC] * (len(args) - scalars),
        out_specs=[VMEM_SPEC] * len(outs),
        scratch_shapes=scratch,
        compiler_params=pltpu.CompilerParams(
            collective_id=collective_id, has_side_effects=True, vmem_limit_bytes=62 * 2**20
        ),
        name=name,
    )(*args)


def shaped(shape, dtype):
    return jax.ShapeDtypeStruct(shape, dtype)


def pair_roles(size):
    me = lax.axis_index("dp")
    partner = me + 1 - 2 * lax.rem(me, 2)
    far = [(lax.rem(me + 2 * step, size), lax.rem(me + size - 2 * step, size)) for step in range(1, size // 2)]
    return me, partner, far


def pair_group(size):
    me, partner, far = pair_roles(size)
    return [(partner, {"dp": partner})] + [(to, {"dp": to}) for to, _ in far]


def remote(source, target, send, recv, where):
    return pltpu.make_async_remote_copy(
        src_ref=source, dst_ref=target, send_sem=send, recv_sem=recv, device_id=where, device_id_type=MESH
    )


def pair_sems(size):
    return sems(1) + sems(max(1, size // 2 - 1)) * 2


def gather_start(size, own_ref, place, sem):
    me, partner, far = pair_roles(size)
    near = remote(own_ref, place(me), sem[0].at[0], sem[1].at[0], {"dp": partner})
    wide = [
        remote(own_ref, place(me), sem[2].at[step], sem[3].at[step], {"dp": to})
        for step, (to, _) in enumerate(far)
    ]
    for copy in wide + [near]:
        copy.start()
    return near, wide


def gather_pass(size, copies, place, sem):
    me, partner, far = pair_roles(size)
    passed = []
    for step, (_, origin) in enumerate(far):
        copies[1][step].wait()
        passed.append(
            remote(place(origin), place(origin), sem[4].at[step], sem[5].at[step], {"dp": partner})
        )
        passed[-1].start()
    return [copies[0]] + passed


LAG = 4
CHUNK = 32


def line_roles(size):
    me = lax.axis_index("tensor")
    lower, upper = lax.rem(me + size - 1, size), lax.rem(me + 1, size)
    return [(me, lower, upper), (size - 1 - me, upper, lower)]


def greet_line(size, groups):
    me = lax.axis_index("tensor")
    barrier = pltpu.get_barrier_semaphore()

    @pl.when(me > 0)
    def _():
        pl.semaphore_signal(barrier, inc=1, device_id={"tensor": me - 1}, device_id_type=MESH)

    @pl.when(me < size - 1)
    def _():
        pl.semaphore_signal(barrier, inc=1, device_id={"tensor": me + 1}, device_id_type=MESH)

    total = 0
    for group in groups:
        for _, where in group:
            pl.semaphore_signal(barrier, inc=1, device_id=where, device_id_type=MESH)
            total += 1

    beside = jnp.where(me > 0, 1, 0) + jnp.where(me < size - 1, 1, 0)
    pl.semaphore_wait(barrier, total + beside)


def both(*conditions):
    return functools.reduce(jnp.logical_and, conditions)


def line_start(size, part, slots, sem):
    count = part.shape[1]
    for flow, (place, toward, _) in enumerate(line_roles(size)):

        @pl.when(place == size - 1)
        def _(flow=flow, toward=toward):
            @pl.loop(0, count)
            def _(k):
                remote(
                    part.at[flow, k], slots.at[flow, k], sem[0].at[flow, k], sem[1].at[flow, k], {"tensor": toward}
                ).start()


def line_start_block(size, part, slots, sem, flow, begin, count):
    me = lax.axis_index("tensor")
    lower, upper = lax.rem(me + size - 1, size), lax.rem(me + 1, size)
    place = jnp.where(flow == 0, me, size - 1 - me)
    toward = jnp.where(flow == 0, lower, upper)

    @pl.when(place == size - 1)
    def _():
        @pl.loop(0, count)
        def _(step):
            k = begin + step
            remote(
                part.at[flow, k], slots.at[flow, k], sem[0].at[flow, k], sem[1].at[flow, k], {"tensor": toward}
            ).start()


def line_run(size, part, slots, sums, full, sem, finish, between=(), work=None):
    count = part.shape[1]
    roles = line_roles(size)

    def reduce_copy(flow, k, source):
        return remote(
            source.at[flow, k], slots.at[flow, k], sem[0].at[flow, k], sem[1].at[flow, k], {"tensor": roles[flow][1]}
        )

    def spread_copy(flow, k):
        return remote(
            full.at[flow, k], full.at[flow, k], sem[2].at[flow, k], sem[3].at[flow, k], {"tensor": roles[flow][2]}
        )

    def one_step(step):
        if work is not None:
            work(step)

        for flow, (place, _, _) in enumerate(roles):
            k = step - LAG * (size - 1 - place)
            inside = both(k >= 0, k < count)

            @pl.when(both(inside, place > 0, place < size - 1))
            def _(flow=flow, k=k):
                reduce_copy(flow, k, sums).wait_recv()
                sums[flow, k] = (slots[flow, k].astype(F32) + part[flow, k].astype(F32)).astype(BF16)
                reduce_copy(flow, k, sums).start()

            @pl.when(both(inside, place == 0))
            def _(flow=flow, k=k):
                reduce_copy(flow, k, sums).wait_recv()
                full[flow, k] = finish(flow, k, slots[flow, k].astype(F32) + part[flow, k].astype(F32))
                spread_copy(flow, k).start()

        for flow, (place, _, _) in enumerate(roles):
            k = step - LAG * (size - 1) - LAG * place
            inside = both(k >= 0, k < count, place > 0)

            @pl.when(inside)
            def _(flow=flow, k=k):
                spread_copy(flow, k).wait_recv()

            @pl.when(both(inside, place < size - 1))
            def _(flow=flow, k=k):
                spread_copy(flow, k).start()

    begun, last = 0, count + 2 * LAG * (size - 1)
    for stop, action in tuple(between) + ((last, None),):
        stop = min(stop, last)
        pl.loop(begun, stop)(one_step)
        begun = stop
        if action is not None:
            action()

    for flow, (place, _, _) in enumerate(roles):

        @pl.when(place > 0)
        def _(flow=flow):
            @pl.loop(0, count)
            def _(k):
                reduce_copy(flow, k, sums).wait_send()

        @pl.when(place < size - 1)
        def _(flow=flow):
            @pl.loop(0, count)
            def _(k):
                spread_copy(flow, k).wait_send()


def spread_start(size, mine, full, sem):
    for flow, (place, _, away) in enumerate(line_roles(size)):

        @pl.when(place == 0)
        def _(flow=flow, away=away):
            @pl.loop(0, mine.shape[0])
            def _(k):
                remote(
                    mine.at[k], full.at[flow, k], sem[0].at[flow, k], sem[1].at[flow, k], {"tensor": away}
                ).start()
                full[flow, k] = mine[k]


def spread_copy(size, flow, k, full, sem):
    toward = line_roles(size)[flow][2]
    return remote(full.at[flow, k], full.at[flow, k], sem[0].at[flow, k], sem[1].at[flow, k], {"tensor": toward})


def spread_steps(size, mine, full, sem, begin, end):
    count = mine.shape[0]

    @pl.loop(begin, end)
    def _(step):
        for flow, (place, _, _) in enumerate(line_roles(size)):
            k = step - SPREAD_LAG * place
            inside = both(k >= 0, k < count, place > 0)

            @pl.when(inside)
            def _(flow=flow, k=k):
                spread_copy(size, flow, k, full, sem).wait_recv()

            @pl.when(both(inside, place < size - 1))
            def _(flow=flow, k=k):
                spread_copy(size, flow, k, full, sem).start()


def spread_end(size, mine, full, sem):
    for flow, (place, _, _) in enumerate(line_roles(size)):

        @pl.when(place < size - 1)
        def _(flow=flow):
            @pl.loop(0, mine.shape[0])
            def _(k):
                spread_copy(size, flow, k, full, sem).wait_send()


def line_sems(count, kinds):
    return [DMA((2, count))] * kinds


def add_row(vector_ref, index, value):
    vector_ref[index : index + 1] += jnp.sum(value, axis=0, keepdims=True)


CONTRACT_LAST = (((1,), (1,)), ((), ()))
CONTRACT_FIRST = (((0,), (0,)), ((), ()))


PIECES = 4
GROUP = 4
ROW_BLOCK = 256
SPREAD_LAG = 2


def matmul(left, right):
    return jnp.dot(left, right, preferred_element_type=F32)


def matmul_last(left, right):
    return lax.dot_general(left, right, CONTRACT_LAST, preferred_element_type=F32)


def matmul_first(left, right):
    return lax.dot_general(left, right, CONTRACT_FIRST, preferred_element_type=F32)


def part_rows(index, count):
    return pl.ds(pl.multiple_of(index * count, count), count)


def block_of(step, group):
    return lax.rem(step, 2), lax.div(step, 2) * group


def gather_kernel(sizes, tokens, qkv, proj, wide_tokens, wide_qkv, wide_proj, *sem):
    data, blocks, ranks = sizes["dp"], sizes["ctx"], sizes["tensor"]
    me, rank = lax.axis_index("ctx"), lax.axis_index("tensor")
    mate = rank + 1 - 2 * lax.rem(rank, 2)
    peers = peers_of("ctx", blocks)
    piece = qkv.shape[1]
    rows = tokens.shape[0] // 2 // PIECES

    def span(parity, index):
        return pl.ds(pl.multiple_of((parity * PIECES + index) * rows, rows), rows)

    own_half = lax.rem(rank, 2)
    greet([peers, [(mate, {"tensor": mate})], pair_group(data)])
    across = []
    for index in range(PIECES):
        for step, (_, where) in enumerate(peers):
            here = span(own_half, index)
            across.append(
                remote(tokens.at[here], wide_tokens.at[me, here], sem[0].at[step, index], sem[1].at[step, index], where)
            )
            across[-1].start()
    place_qkv = lambda index: wide_qkv.at[:, part_rows(index, piece)]
    place_proj = lambda index: wide_proj.at[index]
    copies = gather_start(data, qkv, place_qkv, sem[4:10])
    projs = gather_start(data, proj, place_proj, sem[10:16])
    mine = lax.axis_index("dp")
    wide_qkv[:, part_rows(mine, piece)] = qkv[...]
    wide_proj[mine] = proj[...]
    wide_tokens[me] = tokens[...]
    passed = []
    for index in range(PIECES):
        for step in range(len(peers)):
            origin = lax.rem(me + blocks - step - 1, blocks)
            across[index * len(peers) + step].wait_recv()
            here = span(own_half, index)
            place = wide_tokens.at[origin, here]
            passed.append(
                remote(place, place, sem[2].at[step, index], sem[3].at[step, index], {"tensor": mate})
            )
            passed[-1].start()
    passing = gather_pass(data, copies, place_qkv, sem[4:10])
    passing += gather_pass(data, projs, place_proj, sem[10:16])
    for copy in across:
        copy.wait_send()
    wait_all(passed)
    wait_all(passing)


def forward_kernel(
    sizes, score_scale, length_ref, tokens, wide_tokens, wide_qkv, wide_proj, *refs
):
    given, (q_ref, k_ref, v_ref, out_ref, low_ref, log_ref, part_ref, proj_ref, flat_ref, fixed) = refs[:-10], refs[-10:]
    length = length_ref[0]
    for index, vector in enumerate(given):
        fixed[index : index + 1, : vector.shape[0]] = vector[...].reshape(1, -1)
    rows, width = q_ref.shape
    keys = k_ref.shape[0]
    block = math.gcd(rows, ROW_BLOCK)
    column = wide_proj.shape[2]
    for index in range(sizes["dp"]):
        proj_ref[:, index * column : (index + 1) * column] = wide_proj[index]
    for slot, index in enumerate((1, 2, 0)):
        flat_ref[:, slot * width : (slot + 1) * width] = wide_qkv[index]

    @pl.loop(0, keys // block)
    def _(step):
        here = part_rows(step, block)
        found = wide_tokens[here]
        k_ref[here] = matmul(found, wide_qkv[1]).astype(BF16)
        v_ref[here] = (matmul(found, wide_qkv[2]) + fixed[8:9, :width]).astype(BF16)

    hidden_keys = lax.broadcasted_iota(jnp.int32, (block, keys), 1) >= length

    @pl.loop(0, rows // block)
    def _(step):
        here = part_rows(step, block)
        q_ref[here] = (matmul(tokens[here], wide_qkv[0]) + fixed[7:8, :width]).astype(BF16)
        for head in range(width // HD):
            lanes = slice(head * HD, (head + 1) * HD)
            scores = matmul_last(q_ref[here, lanes], k_ref[:, lanes]) * score_scale
            scores = jnp.where(hidden_keys, NEGATIVE, scores)
            top = jnp.max(scores, axis=-1, keepdims=True)
            weights = jnp.exp(scores - top)
            total = jnp.sum(weights, axis=-1, keepdims=True)
            attended = matmul(weights.astype(BF16), v_ref[:, lanes]) / total
            out_ref[here, lanes] = attended
            low_ref[here, lanes] = attended.astype(BF16)
            log_ref[here, head : head + 1] = top + jnp.log(total)
        part_ref[here] = matmul(low_ref[here], proj_ref[...]).astype(BF16)


def near_start(size, grads, chip, sem):
    _, partner, _ = pair_roles(size)
    piece = chip.shape[1]
    copies = [
        remote(
            grads.at[part_rows(2 * index + lax.rem(partner, 2), piece)],
            chip.at[index],
            sem[0].at[index],
            sem[1].at[index],
            {"dp": partner},
        )
        for index in range(size // 2)
    ]
    for copy in copies:
        copy.start()
    return copies


def far_start(size, copies, grads, chip, merged, slots, sem):
    me, _, far = pair_roles(size)
    piece = chip.shape[1]
    wait_all(copies)
    for index in range(size // 2):
        own = grads[part_rows(2 * index + lax.rem(me, 2), piece)]
        merged[index] = (own.astype(F32) + chip[index].astype(F32)).astype(BF16)
    moving = [
        remote(
            merged.at[lax.div(to, 2)], slots.at[lax.div(me, 2)], sem[2].at[step], sem[3].at[step], {"dp": to}
        )
        for step, (to, _) in enumerate(far)
    ]
    for copy in moving:
        copy.start()
    slots[lax.div(me, 2)] = merged[lax.div(me, 2)]
    return moving


def blocks_start(sizes, value, blocks, sem):
    me = lax.axis_index("ctx")
    blocks[me] = value
    return send_all(
        lambda other: (blocks.at[me], blocks.at[me]), peers_of("ctx", sizes["ctx"]), sem[0], sem[1]
    )


def middle_kernel(
    sizes, part, tokens, cotangent, fixed, up, down,
    attn_low, attn_ref, output_ref, vector_ref, block_up, block_down,
    wide_up, wide_down, low, normed_ref, inverse_ref, out_ref, pre, hidden,
    part_two, back_ref, second_low, d_pre, part_three, grads_up, grads_down,
    slots, sums, slots_two, sums_two, slots_three, sums_three,
    chip_a, chip_b, merged_a, merged_b, far_a, far_b, *sem
):
    size, data = sizes["tensor"], sizes["dp"]
    mine = lax.axis_index("dp")
    piece = up.shape[0]
    chunks, chunk, model = part.shape[1:]
    group = math.gcd(chunks, GROUP)
    count = group * chunk
    steps = 2 * chunks // group
    line_one, line_two, line_three = sem[0:4], sem[4:8], sem[8:12]
    sem_up, sem_down = sem[12:18], sem[18:24]
    sem_a, sem_b = sem[24:28], sem[28:32]
    greet_line(size, [pair_group(data)])
    line_start(size, part, slots, line_one)
    place_up = lambda index: wide_up.at[part_rows(index, piece)]
    place_down = lambda index: wide_down.at[part_rows(index, piece)]
    ups = gather_start(data, up, place_up, sem_up)
    downs = gather_start(data, down, place_down, sem_down)
    wide_up[part_rows(mine, piece)] = up[...]
    wide_down[part_rows(mine, piece)] = down[...]
    vector_ref[...] = jnp.zeros_like(vector_ref)

    def first_finish(flow, k, total):
        first_sum = tokens[flow, k].astype(F32) + total + fixed[0:1, :model]
        first_out, normed, inverse = layer_norm(first_sum, fixed[1:2, :model], fixed[2:3, :model])
        out_ref[k] = first_out
        normed_ref[k] = normed
        inverse_ref[k] = inverse
        return first_out.astype(BF16)

    passed = []

    def hand_over():
        passed.extend(gather_pass(data, ups, place_up, sem_up))
        passed.extend(gather_pass(data, downs, place_down, sem_down))

    line_run(size, part, slots, sums, low, line_one, first_finish, [(LAG * size, hand_over)])
    wait_all(passed)

    @pl.loop(0, steps)
    def _(step):
        flow, begin = block_of(step, group)
        here = pl.ds(pl.multiple_of(step * count, count), count)
        found = low[flow, pl.ds(begin, group)].reshape(count, model)
        value = matmul(found, wide_up[...]) + fixed[6:7, : pre.shape[1]]
        pre[here] = value
        hidden[here] = gelu_value(value).astype(BF16)
        result = matmul_last(hidden[here], wide_down[...]).astype(BF16)
        part_two[flow, pl.ds(begin, group)] = result.reshape(group, chunk, model)
        line_start_block(size, part_two, slots_two, line_two, flow, begin, group)

    def second_finish(flow, k, total):
        second_sum = out_ref[k] + total + fixed[3:4, :model]
        result, normed, inverse = layer_norm(second_sum, fixed[4:5, :model], fixed[5:6, :model])
        upstream = cotangent[flow, k].astype(F32)
        d_second = norm_back(upstream, normed, inverse, fixed[4:5, :model])
        output_ref[k] = result.astype(BF16)
        back_ref[k] = d_second
        add_row(vector_ref, 0, upstream)
        add_row(vector_ref, 1, upstream * normed)
        add_row(vector_ref, 2, d_second)
        return d_second.astype(BF16)

    def slope_work(step):
        @pl.when(step < 2 * chunks)
        def _():
            here = part_rows(step, chunk)
            pre[here] = gelu_slope(pre[here])

    line_run(size, part_two, slots_two, sums_two, second_low, line_two, second_finish, work=slope_work)

    @pl.loop(0, steps)
    def _(step):
        flow, begin = block_of(step, group)
        here = pl.ds(pl.multiple_of(step * count, count), count)
        found = second_low[flow, pl.ds(begin, group)].reshape(count, model)
        value = matmul(found, wide_down[...]) * pre[here]
        add_row(vector_ref, 6, value)
        d_pre[here] = value.astype(BF16)
        result = matmul_last(d_pre[here], wide_up[...]).astype(BF16)
        part_three[flow, pl.ds(begin, group)] = result.reshape(group, chunk, model)
        line_start_block(size, part_three, slots_three, line_three, flow, begin, group)

    def third_finish(flow, k, total):
        d_first = total + back_ref[k]
        normed = normed_ref[k]
        d_attn = norm_back(d_first, normed, inverse_ref[k], fixed[1:2, :model])
        attn_ref[k] = d_attn
        add_row(vector_ref, 3, d_first)
        add_row(vector_ref, 4, d_first * normed)
        add_row(vector_ref, 5, d_attn)
        return d_attn.astype(BF16)

    pieces = model // 128

    def grads_work(step):
        @pl.when(step < pieces)
        def _():
            columns = part_rows(step, 128)
            left = [
                second_low[block % 2, block // 2 * group : block // 2 * group + group, :, columns].reshape(count, 128)
                for block in range(steps)
            ]
            grads_down[columns] = matmul_first(jnp.concatenate(left, axis=0), hidden[...]).astype(BF16)

        @pl.when(jnp.logical_and(step >= pieces, step < 2 * pieces))
        def _():
            columns = part_rows(step - pieces, 128)
            left = [
                low[block % 2, block // 2 * group : block // 2 * group + group, :, columns].reshape(count, 128)
                for block in range(steps)
            ]
            grads_up[columns] = matmul_first(jnp.concatenate(left, axis=0), d_pre[...]).astype(BF16)

    near_a, near_b, moving_a, moving_b = [], [], [], []

    def near_down():
        near_b.extend(near_start(data, grads_down, chip_b, sem_b))

    def near_up():
        near_a.extend(near_start(data, grads_up, chip_a, sem_a))
        moving_b.extend(far_start(data, near_b, grads_down, chip_b, merged_b, far_b, sem_b))

    def far_up():
        moving_a.extend(far_start(data, near_a, grads_up, chip_a, merged_a, far_a, sem_a))

    between = [(pieces, near_down), (2 * pieces, near_up), (2 * pieces + LAG, far_up)]
    line_run(
        size, part_three, slots_three, sums_three, attn_low, line_three, third_finish, between, work=grads_work
    )
    wait_all(moving_b)
    block_down[...] = slot_sum(far_b, data // 2).astype(BF16)
    wait_all(moving_a)
    block_up[...] = slot_sum(far_a, data // 2).astype(BF16)


def back_kernel(
    sizes, score_scale, length_ref, q_ref, k_ref, v_ref, attended_ref, low_ref, log_ref,
    proj_ref, attn_low, tokens, vectors, flat, d_attn, block_a, block_b, mine,
    full, output_ref, owned, owned_a, owned_b, vector_ref,
    dk_ref, dv_ref, heads_ref, stack, grads, own_ref,
    part, slots, sums, keys, total_ref, chip, merged, far, blocks, blocks_a, blocks_b, slots_v, grid_v, *sem
):
    size, data = sizes["tensor"], sizes["dp"]
    rank, me = lax.axis_index("tensor"), lax.axis_index("ctx")
    chunks, chunk, model = part.shape[1:]
    group = math.gcd(chunks, GROUP)
    count = group * chunk
    steps = 2 * chunks // group
    wide = keys.shape[2]
    line, spread, sem_keys, sem_grads = sem[0:4], sem[4:6], sem[6:8], sem[8:12]
    sem_small, sem_grid, sem_a, sem_b, sem_last = sem[12:14], sem[14:16], sem[16:18], sem[18:20], sem[20:22]
    others = peers_of("ctx", sizes["ctx"])
    here_v, everyone = grid_peers(sizes)
    peers = peers_of("tensor", size)
    greet([peers, everyone])
    spread_start(size, mine, output_ref, spread)
    moving_a = blocks_start(sizes, block_a[...], blocks_a, sem_a)
    moving_b = blocks_start(sizes, block_b[...], blocks_b, sem_b)

    length = length_ref[0]
    rows, width = q_ref.shape
    total_keys = k_ref.shape[0]
    block = math.gcd(rows, ROW_BLOCK)
    hidden_keys = lax.broadcasted_iota(jnp.int32, (block, total_keys), 1) >= length
    dk_ref[...] = jnp.zeros_like(dk_ref)
    dv_ref[...] = jnp.zeros_like(dv_ref)
    own_ref[...] = vectors[...]
    stack[:, :, 2 * width :] = jnp.zeros((sizes["ctx"], rows, width), BF16)
    heads = width // HD
    turns = rows // block * heads
    relays = mine.shape[0] + SPREAD_LAG * (size - 1)

    @pl.loop(0, rows // block)
    def _(step):
        here = part_rows(step, block)
        heads_ref[here] = matmul_last(attn_low[here], proj_ref[...]).astype(BF16)
        for head in range(heads):
            lanes = slice(head * HD, (head + 1) * HD)
            q, k, v, d_heads = q_ref[here, lanes], k_ref[:, lanes], v_ref[:, lanes], heads_ref[here, lanes]
            delta = jnp.sum(d_heads.astype(F32) * attended_ref[here, lanes], axis=-1, keepdims=True)
            scores = matmul_last(q, k) * score_scale
            scores = jnp.where(hidden_keys, NEGATIVE, scores)
            probs = jnp.exp(scores - log_ref[here, head : head + 1])
            d_scores = (probs * (matmul_last(d_heads, v) - delta)).astype(BF16)
            dv_ref[:, lanes] += matmul_first(probs.astype(BF16), d_heads)
            dk_ref[:, lanes] += matmul_first(d_scores, q) * score_scale
            d_query = matmul(d_scores, k) * score_scale
            own_ref[7:8, lanes] += jnp.sum(d_query, axis=0, keepdims=True)
            stack[me, here, 2 * width + head * HD : 2 * width + (head + 1) * HD] = d_query.astype(BF16)
            turn = step * heads + head
            spread_steps(size, mine, output_ref, spread, turn * relays // turns, (turn + 1) * relays // turns)

    own_ref[7:8, width : 2 * width] = jnp.sum(dv_ref[...], axis=0, keepdims=True)
    stack[:, :, :width] = dk_ref[...].astype(BF16).reshape(sizes["ctx"], rows, width)
    stack[:, :, width : 2 * width] = dv_ref[...].astype(BF16).reshape(sizes["ctx"], rows, width)

    def span(step):
        flow, begin = step % 2, step // 2 * group
        return slice((flow * chunks + begin) * chunk, (flow * chunks + begin) * chunk + count)

    moving_keys = [
        [
            remote(
                stack.at[other, span(step), 0:wide],
                keys.at[me, span(step)],
                sem_keys[0].at[index, step],
                sem_keys[1].at[index, step],
                where,
            )
            for index, (other, where) in enumerate(others)
        ]
        for step in range(steps)
    ]
    for copies in moving_keys:
        for copy in copies:
            copy.start()
    small = send_all(lambda other: (own_ref, slots_v.at[rank]), peers, sem_small[0], sem_small[1])
    slots_v[rank] = own_ref[...]

    @pl.loop(0, model // 128)
    def _(index):
        columns = part_rows(index, 128)
        every = stack[...].reshape(total_keys, 3 * width)
        grads[columns, : 3 * width] = matmul_first(tokens[:, columns], every).astype(BF16)
        grads[columns, 3 * width :] = matmul_first(attn_low[:, columns], low_ref[...]).astype(BF16)

    near = near_start(data, grads, chip, sem_grads)
    state = {}

    def send_group(step):
        flow, begin = step % 2, step // 2 * group
        there = span(step)
        keys[me, there] = stack[me, there, 0:wide]
        for copy in moving_keys[step]:
            copy.wait_recv()
        total = keys[0, there].astype(F32)
        for index in range(1, sizes["ctx"]):
            total = total + keys[index, there].astype(F32)
        total_ref[there, 0:wide] = total.astype(BF16)
        total_ref[there, wide:] = stack[me, there, wide:]
        result = matmul_last(total_ref[there], flat[...]).astype(BF16)
        part[flow, begin : begin + group] = result.reshape(group, chunk, model)
        line_start_block(size, part, slots, line, flow, begin, group)

    def go_far():
        state["far"] = far_start(data, near, grads, chip, merged, far, sem_grads)
        wait_all(small)
        own = own_ref[...]
        row_ids = lax.broadcasted_iota(jnp.int32, own.shape, 0)
        grid_v[here_v] = jnp.where(row_ids < 6, slot_sum(slots_v, size), own)
        state["small"] = send_all(
            lambda other: (grid_v.at[here_v], grid_v.at[here_v]), everyone, sem_grid[0], sem_grid[1]
        )

    def go_across():
        wait_all(state["far"])
        value = slot_sum(far, data // 2).astype(BF16)
        state["across"] = blocks_start(sizes, value, blocks, sem_last)

    def finish(flow, k, total):
        return (total + d_attn[k]).astype(BF16)

    for step in range(2):
        send_group(step)
    between = [(1, go_far)]
    between += [(LAG + 2 * step - 3, functools.partial(send_group, step)) for step in range(2, steps)]
    between += [(max(LAG * size, LAG + 2 * steps), go_across)]
    line_run(size, part, slots, sums, full, line, finish, between)
    spread_end(size, mine, output_ref, spread)
    for copies in moving_keys:
        for copy in copies:
            copy.wait_send()
    wait_all(state["small"])
    vector_ref[...] = slot_sum(grid_v, data * sizes["ctx"])
    wait_all(moving_a)
    owned_a[...] = slot_sum(blocks_a, sizes["ctx"])
    wait_all(moving_b)
    owned_b[...] = slot_sum(blocks_b, sizes["ctx"])
    wait_all(state["across"])
    owned[...] = slot_sum(blocks, sizes["ctx"])


def unpack_kernel(
    full, output, owned, owned_a, owned_b, sums,
    output_ref, tokens_ref, qkv_ref, proj_ref, up_ref, down_ref, query_ref, value_ref, *rows
):
    width = qkv_ref.shape[2]
    output_ref[...] = output[...]
    tokens_ref[...] = full[...].astype(F32)
    for index, slot in enumerate((2, 0, 1)):
        qkv_ref[index] = owned[:, slot * width : (slot + 1) * width]
    proj_ref[...] = owned[:, 3 * width :].T
    up_ref[...] = owned_a[...]
    down_ref[...] = owned_b[...]
    query_ref[...] = sums[7, :width]
    value_ref[...] = sums[7, width : 2 * width]
    for index, row in enumerate(rows):
        row[...] = sums[index, : row.shape[0]]


def local_call(kernel, outs, scratch, args, name, scalars=1):
    return pl.pallas_call(
        kernel,
        out_shape=outs,
        in_specs=[pl.BlockSpec(memory_space=pltpu.SMEM)] * scalars + [VMEM_SPEC] * (len(args) - scalars),
        out_specs=[VMEM_SPEC] * len(outs),
        scratch_shapes=scratch,
        compiler_params=pltpu.CompilerParams(vmem_limit_bytes=60 * 2**20),
        name=name,
    )(*args)


def per_device(
    sizes,
    tokens,
    lengths,
    cotangent,
    qkv_weight,
    query_bias,
    value_bias,
    proj_weight,
    proj_bias,
    first_gain,
    first_shift,
    up_weight,
    up_bias,
    down_weight,
    down_bias,
    second_gain,
    second_shift,
):
    data, blocks, ranks = sizes["dp"], sizes["ctx"], sizes["tensor"]
    rows_in = tokens[0]
    row_count, model = rows_in.shape
    half = row_count // 2
    chunk = math.gcd(half, CHUNK)
    chunks = half // chunk
    piece, width = qkv_weight.shape[1:]
    up_width = up_weight.shape[1]
    keys = blocks * row_count
    score_scale = 1.0 / math.sqrt(HD)
    split = (2, chunks, chunk, model)
    flow = pltpu.VMEM(split, BF16)
    line = line_sems(chunks, 4)
    local = shaped(split[1:], F32)
    held = pltpu.VMEM(split[1:], F32)
    steps = 2 * chunks // math.gcd(chunks, GROUP)
    vector_width = max(model, up_width, 2 * width)
    given = (
        proj_bias, first_gain, first_shift, down_bias, second_gain, second_shift, up_bias, query_bias, value_bias
    )

    wide_tokens, wide_qkv, wide_proj = call(
        functools.partial(gather_kernel, sizes),
        [
            shaped((blocks, row_count, model), BF16),
            shaped((3, model, width), BF16),
            shaped((data,) + proj_weight.shape, BF16),
        ],
        [DMA((blocks - 1, PIECES))] * 4 + pair_sems(data) * 2,
        0,
        (rows_in, qkv_weight, proj_weight),
        "gather_inputs",
    )
    wide_tokens = wide_tokens.reshape(keys, model)
    queries, key_rows, value_rows, attended, attended_low, log_total, attn_part, flat_proj, flat_qkv, fixed = local_call(
        functools.partial(forward_kernel, sizes, score_scale),
        [
            shaped((row_count, width), BF16),
            shaped((keys, width), BF16),
            shaped((keys, width), BF16),
            shaped((row_count, width), F32),
            shaped((row_count, width), BF16),
            shaped((row_count, width // HD), F32),
            shaped((row_count, model), BF16),
            shaped((width, model), BF16),
            shaped((model, 3 * width), BF16),
            shaped((16, vector_width), F32),
        ],
        [],
        (lengths, rows_in, wide_tokens, wide_qkv, wide_proj) + given,
        "attention_forward",
    )

    up_shape = (model, up_width)
    pair_slots = pltpu.VMEM((data // 2, model // data, up_width), BF16)
    pair_moves = sems(data // 2) + sems(max(1, data // 2 - 1))
    attn_low, d_attn, output_part, vectors, block_up, block_down = call(
        functools.partial(middle_kernel, sizes),
        [
            shaped(split, BF16),
            local,
            shaped(split[1:], BF16),
            shaped((8, vector_width), F32),
            shaped((model // data, up_width), BF16),
            shaped((model // data, up_width), BF16),
        ],
        [
            pltpu.VMEM(up_shape, BF16),
            pltpu.VMEM(up_shape, BF16),
            flow,
            held,
            pltpu.VMEM((chunks, chunk, 1), F32),
            held,
            pltpu.VMEM((row_count, up_width), F32),
            pltpu.VMEM((row_count, up_width), BF16),
            flow,
            held,
            flow,
            pltpu.VMEM((row_count, up_width), BF16),
            flow,
            pltpu.VMEM(up_shape, BF16),
            pltpu.VMEM(up_shape, BF16),
        ]
        + [flow] * 6
        + [pair_slots] * 6
        + line * 3
        + pair_sems(data) * 2
        + pair_moves * 2,
        1,
        (
            attn_part.reshape(split),
            rows_in.reshape(split),
            cotangent[0].reshape(split),
            fixed,
            up_weight,
            down_weight.T,
        ),
        "norms_and_hidden",
    )

    own_shape = (model // data, 4 * width)
    last_pair = pltpu.VMEM((data // 2,) + own_shape, BF16)
    grad_tokens, output, own_last, own_up, own_down, sums = call(
        functools.partial(back_kernel, sizes, score_scale),
        [
            shaped(split, BF16),
            shaped(split, BF16),
            shaped(own_shape, F32),
            shaped((model // data, up_width), F32),
            shaped((model // data, up_width), F32),
            shaped(vectors.shape, F32),
        ],
        [
            pltpu.VMEM((keys, width), F32),
            pltpu.VMEM((keys, width), F32),
            pltpu.VMEM((row_count, width), BF16),
            pltpu.VMEM((blocks, row_count, 3 * width), BF16),
            pltpu.VMEM((model, 4 * width), BF16),
            pltpu.VMEM(vectors.shape, F32),
        ]
        + [flow] * 3
        + [
            pltpu.VMEM((blocks, row_count, 2 * width), BF16),
            pltpu.VMEM((row_count, 3 * width), BF16),
        ]
        + [last_pair] * 3
        + [pltpu.VMEM((blocks,) + own_shape, BF16)]
        + [pltpu.VMEM((blocks, model // data, up_width), BF16)] * 2
        + [
            pltpu.VMEM((ranks,) + vectors.shape, F32),
            pltpu.VMEM((data * blocks,) + vectors.shape, F32),
        ]
        + line
        + line_sems(chunks, 2)
        + [DMA((max(1, blocks - 1), steps))] * 2
        + pair_moves
        + sems(ranks - 1)
        + sems(data * blocks - 1)
        + sems(blocks - 1) * 3,
        2,
        (
            lengths, queries, key_rows, value_rows, attended, attended_low, log_total,
            flat_proj, attn_low.reshape(row_count, model), wide_tokens, vectors,
            flat_qkv, d_attn, block_up, block_down, output_part,
        ),
        "attention_backward",
        scalars=1,
    )
    output, grad_tokens, own_qkv, own_proj, own_up, own_down, grad_query, grad_value, *rows = local_call(
        unpack_kernel,
        [
            shaped((row_count, model), BF16),
            shaped((row_count, model), F32),
            shaped((3, model // data, width), F32),
            shaped((width, model // data), F32),
            shaped(own_up.shape, F32),
            shaped(own_down.shape, F32),
            shaped((width,), F32),
            shaped((width,), F32),
        ]
        + [shaped((model,), F32)] * 6
        + [shaped((up_width,), F32)],
        [],
        (
            grad_tokens.reshape(row_count, model),
            output.reshape(row_count, model),
            own_last,
            own_up,
            own_down,
            sums,
        ),
        "unpack",
        scalars=0,
    )
    return (
        output[None],
        grad_tokens[None],
        own_qkv,
        grad_query,
        grad_value,
        own_proj,
        rows[5],
        rows[4],
        rows[3],
        own_up,
        rows[6],
        own_down.T,
        rows[2],
        rows[1],
        rows[0],
    )


def solution(mesh):
    placed = (
        P("dp", "ctx", None),
        P("dp"),
        P("dp", "ctx", None),
        P(None, "dp", "tensor"),
        P("tensor"),
        P("tensor"),
        P("tensor", "dp"),
        P(),
        P(),
        P(),
        P("dp", "tensor"),
        P("tensor"),
        P("tensor", "dp"),
        P(),
        P(),
        P(),
    )
    return jax.shard_map(
        functools.partial(per_device, dict(mesh.shape)),
        mesh=mesh,
        in_specs=placed,
        out_specs=(
            P("dp", "ctx", None),
            P("dp", "ctx", None),
            P(None, "dp", "tensor"),
            P("tensor"),
            P("tensor"),
            P("tensor", "dp"),
            P(),
            P(),
            P(),
            P("dp", "tensor"),
            P("tensor"),
            P("tensor", "dp"),
            P(),
            P(),
            P(),
        ),
        check_vma=False,
    )
```

```python
import functools
import math

import jax
import jax.numpy as jnp
from jax import lax
from jax.experimental import pallas as pl
from jax.experimental.pallas import tpu as pltpu
from jax.sharding import PartitionSpec as P

HD = 64


EPSILON = 1e-05
NEGATIVE = -1e30
ROOT_HALF = 0.7071067811865476
ROOT_TWO_PI = 2.5066282746310002
MESH = pl.DeviceIdType.MESH
BF16 = jnp.bfloat16
F32 = jnp.float32
VMEM_SPEC = pl.BlockSpec(memory_space=pltpu.VMEM)
DMA = pltpu.SemaphoreType.DMA


def layer_norm(hidden_in, norm_gain, norm_shift):
    centred = hidden_in - jnp.mean(hidden_in, axis=-1, keepdims=True)
    inverse = lax.rsqrt(jnp.mean(centred * centred, axis=-1, keepdims=True) + EPSILON)
    normed = centred * inverse
    return (normed * norm_gain + norm_shift, normed, inverse)


def norm_back(upstream, normed, inverse, norm_gain):
    scaled = upstream * norm_gain
    return inverse * (
        scaled
        - jnp.mean(scaled, axis=-1, keepdims=True)
        - normed * jnp.mean(scaled * normed, axis=-1, keepdims=True)
    )


def gelu_value(pre_act):
    return 0.5 * pre_act * (1.0 + jax.scipy.special.erf(pre_act * ROOT_HALF))


def gelu_slope(pre_act):
    return (
        0.5 * (1.0 + jax.scipy.special.erf(pre_act * ROOT_HALF))
        + pre_act * jnp.exp(-0.5 * pre_act * pre_act) / ROOT_TWO_PI
    )


def peers_of(axis, size):
    me = lax.axis_index(axis)
    found = []
    for step in range(1, size):
        other = lax.rem(me + step, size)
        found.append((other, {axis: other}))
    return found


def grid_peers(sizes):
    count = sizes["dp"] * sizes["ctx"]
    me = lax.axis_index("dp") * sizes["ctx"] + lax.axis_index("ctx")
    found = []
    for step in range(1, count):
        other = lax.rem(me + step, count)
        found.append((other, {"dp": lax.div(other, sizes["ctx"]), "ctx": lax.rem(other, sizes["ctx"])}))
    return me, found


def greet(groups):
    barrier = pltpu.get_barrier_semaphore()
    total = 0
    for group in groups:
        for _, where in group:
            pl.semaphore_signal(barrier, inc=1, device_id=where, device_id_type=MESH)
            total += 1
    pl.semaphore_wait(barrier, total)


def send_all(pairs, peers, send_sem, recv_sem):
    copies = []
    for step, (other, where) in enumerate(peers):
        source, target = pairs(other)
        copies.append(
            pltpu.make_async_remote_copy(
                src_ref=source,
                dst_ref=target,
                send_sem=send_sem.at[step],
                recv_sem=recv_sem.at[step],
                device_id=where,
                device_id_type=MESH,
            )
        )
        copies[-1].start()
    return copies


def wait_all(copies):
    for copy in copies:
        copy.wait()


def slot_sum(slots, count):
    total = slots[0].astype(F32)
    for index in range(1, count):
        total = total + slots[index].astype(F32)
    return total


def sems(count):
    return [DMA((count,)), DMA((count,))]


def call(kernel, outs, scratch, collective_id, args, name, scalars=0):
    return pl.pallas_call(
        kernel,
        out_shape=outs,
        in_specs=[pl.BlockSpec(memory_space=pltpu.SMEM)] * scalars + [VMEM_SPEC] * (len(args) - scalars),
        out_specs=[VMEM_SPEC] * len(outs),
        scratch_shapes=scratch,
        compiler_params=pltpu.CompilerParams(
            collective_id=collective_id, has_side_effects=True, vmem_limit_bytes=62 * 2**20
        ),
        name=name,
    )(*args)


def shaped(shape, dtype):
    return jax.ShapeDtypeStruct(shape, dtype)


def pair_roles(size):
    me = lax.axis_index("dp")
    partner = me + 1 - 2 * lax.rem(me, 2)
    far = [(lax.rem(me + 2 * step, size), lax.rem(me + size - 2 * step, size)) for step in range(1, size // 2)]
    return me, partner, far


def pair_group(size):
    me, partner, far = pair_roles(size)
    return [(partner, {"dp": partner})] + [(to, {"dp": to}) for to, _ in far]


def remote(source, target, send, recv, where):
    return pltpu.make_async_remote_copy(
        src_ref=source, dst_ref=target, send_sem=send, recv_sem=recv, device_id=where, device_id_type=MESH
    )


def pair_sems(size):
    return sems(1) + sems(max(1, size // 2 - 1)) * 2


def gather_start(size, own_ref, place, sem):
    me, partner, far = pair_roles(size)
    near = remote(own_ref, place(me), sem[0].at[0], sem[1].at[0], {"dp": partner})
    wide = [
        remote(own_ref, place(me), sem[2].at[step], sem[3].at[step], {"dp": to})
        for step, (to, _) in enumerate(far)
    ]
    for copy in wide + [near]:
        copy.start()
    return near, wide


def gather_pass(size, copies, place, sem):
    me, partner, far = pair_roles(size)
    passed = []
    for step, (_, origin) in enumerate(far):
        copies[1][step].wait()
        passed.append(
            remote(place(origin), place(origin), sem[4].at[step], sem[5].at[step], {"dp": partner})
        )
        passed[-1].start()
    return [copies[0]] + passed


LAG = 4
CHUNK = 32


def line_roles(size):
    me = lax.axis_index("tensor")
    lower, upper = lax.rem(me + size - 1, size), lax.rem(me + 1, size)
    return [(me, lower, upper), (size - 1 - me, upper, lower)]


def greet_line(size, groups):
    me = lax.axis_index("tensor")
    barrier = pltpu.get_barrier_semaphore()

    @pl.when(me > 0)
    def _():
        pl.semaphore_signal(barrier, inc=1, device_id={"tensor": me - 1}, device_id_type=MESH)

    @pl.when(me < size - 1)
    def _():
        pl.semaphore_signal(barrier, inc=1, device_id={"tensor": me + 1}, device_id_type=MESH)

    total = 0
    for group in groups:
        for _, where in group:
            pl.semaphore_signal(barrier, inc=1, device_id=where, device_id_type=MESH)
            total += 1

    beside = jnp.where(me > 0, 1, 0) + jnp.where(me < size - 1, 1, 0)
    pl.semaphore_wait(barrier, total + beside)


def both(*conditions):
    return functools.reduce(jnp.logical_and, conditions)


def line_start(size, part, slots, sem):
    count = part.shape[1]
    for flow, (place, toward, _) in enumerate(line_roles(size)):

        @pl.when(place == size - 1)
        def _(flow=flow, toward=toward):
            @pl.loop(0, count)
            def _(k):
                remote(
                    part.at[flow, k], slots.at[flow, k], sem[0].at[flow, k], sem[1].at[flow, k], {"tensor": toward}
                ).start()


def line_start_block(size, part, slots, sem, flow, begin, count):
    me = lax.axis_index("tensor")
    lower, upper = lax.rem(me + size - 1, size), lax.rem(me + 1, size)
    place = jnp.where(flow == 0, me, size - 1 - me)
    toward = jnp.where(flow == 0, lower, upper)

    @pl.when(place == size - 1)
    def _():
        @pl.loop(0, count)
        def _(step):
            k = begin + step
            remote(
                part.at[flow, k], slots.at[flow, k], sem[0].at[flow, k], sem[1].at[flow, k], {"tensor": toward}
            ).start()


def line_run(size, part, slots, sums, full, sem, finish, between=(), work=None):
    count = part.shape[1]
    roles = line_roles(size)

    def reduce_copy(flow, k, source):
        return remote(
            source.at[flow, k], slots.at[flow, k], sem[0].at[flow, k], sem[1].at[flow, k], {"tensor": roles[flow][1]}
        )

    def spread_copy(flow, k):
        return remote(
            full.at[flow, k], full.at[flow, k], sem[2].at[flow, k], sem[3].at[flow, k], {"tensor": roles[flow][2]}
        )

    def one_step(step):
        if work is not None:
            work(step)

        for flow, (place, _, _) in enumerate(roles):
            k = step - LAG * (size - 1 - place)
            inside = both(k >= 0, k < count)

            @pl.when(both(inside, place > 0, place < size - 1))
            def _(flow=flow, k=k):
                reduce_copy(flow, k, sums).wait_recv()
                sums[flow, k] = (slots[flow, k].astype(F32) + part[flow, k].astype(F32)).astype(BF16)
                reduce_copy(flow, k, sums).start()

            @pl.when(both(inside, place == 0))
            def _(flow=flow, k=k):
                reduce_copy(flow, k, sums).wait_recv()
                full[flow, k] = finish(flow, k, slots[flow, k].astype(F32) + part[flow, k].astype(F32))
                spread_copy(flow, k).start()

        for flow, (place, _, _) in enumerate(roles):
            k = step - LAG * (size - 1) - LAG * place
            inside = both(k >= 0, k < count, place > 0)

            @pl.when(inside)
            def _(flow=flow, k=k):
                spread_copy(flow, k).wait_recv()

            @pl.when(both(inside, place < size - 1))
            def _(flow=flow, k=k):
                spread_copy(flow, k).start()

    begun, last = 0, count + 2 * LAG * (size - 1)
    for stop, action in tuple(between) + ((last, None),):
        stop = min(stop, last)
        pl.loop(begun, stop)(one_step)
        begun = stop
        if action is not None:
            action()

    for flow, (place, _, _) in enumerate(roles):

        @pl.when(place > 0)
        def _(flow=flow):
            @pl.loop(0, count)
            def _(k):
                reduce_copy(flow, k, sums).wait_send()

        @pl.when(place < size - 1)
        def _(flow=flow):
            @pl.loop(0, count)
            def _(k):
                spread_copy(flow, k).wait_send()


def spread_start(size, mine, full, sem):
    for flow, (place, _, away) in enumerate(line_roles(size)):

        @pl.when(place == 0)
        def _(flow=flow, away=away):
            @pl.loop(0, mine.shape[0])
            def _(k):
                remote(
                    mine.at[k], full.at[flow, k], sem[0].at[flow, k], sem[1].at[flow, k], {"tensor": away}
                ).start()
                full[flow, k] = mine[k]


def spread_copy(size, flow, k, full, sem):
    toward = line_roles(size)[flow][2]
    return remote(full.at[flow, k], full.at[flow, k], sem[0].at[flow, k], sem[1].at[flow, k], {"tensor": toward})


def spread_steps(size, mine, full, sem, begin, end):
    count = mine.shape[0]

    @pl.loop(begin, end)
    def _(step):
        for flow, (place, _, _) in enumerate(line_roles(size)):
            k = step - SPREAD_LAG * place
            inside = both(k >= 0, k < count, place > 0)

            @pl.when(inside)
            def _(flow=flow, k=k):
                spread_copy(size, flow, k, full, sem).wait_recv()

            @pl.when(both(inside, place < size - 1))
            def _(flow=flow, k=k):
                spread_copy(size, flow, k, full, sem).start()


def spread_end(size, mine, full, sem):
    for flow, (place, _, _) in enumerate(line_roles(size)):

        @pl.when(place < size - 1)
        def _(flow=flow):
            @pl.loop(0, mine.shape[0])
            def _(k):
                spread_copy(size, flow, k, full, sem).wait_send()


def line_sems(count, kinds):
    return [DMA((2, count))] * kinds


def add_row(vector_ref, index, value):
    vector_ref[index : index + 1] += jnp.sum(value, axis=0, keepdims=True)


CONTRACT_LAST = (((1,), (1,)), ((), ()))
CONTRACT_FIRST = (((0,), (0,)), ((), ()))


PIECES = 4
GROUP = 4
ROW_BLOCK = 256
SPREAD_LAG = 2


def matmul(left, right):
    return jnp.dot(left, right, preferred_element_type=F32)


def matmul_last(left, right):
    return lax.dot_general(left, right, CONTRACT_LAST, preferred_element_type=F32)


def matmul_first(left, right):
    return lax.dot_general(left, right, CONTRACT_FIRST, preferred_element_type=F32)


def part_rows(index, count):
    return pl.ds(pl.multiple_of(index * count, count), count)


def block_of(step, group):
    return lax.rem(step, 2), lax.div(step, 2) * group


def front_kernel(
    sizes, score_scale, given_count, length_ref, tokens, qkv, proj, cotangent, up, down, *refs
):
    data, blocks, size = sizes["dp"], sizes["ctx"], sizes["tensor"]
    given, refs = refs[:given_count], refs[given_count:]
    q_ref, k_ref, v_ref, out_ref, low_ref, log_ref, proj_ref, flat_ref, wide_tokens = refs[:9]
    middle_outs, refs = refs[9:15], refs[15:]
    wide_qkv, wide_proj, fixed, part = refs[:4]
    middle_scratch, sem = refs[4:31], refs[31:]
    wide_up, wide_down, slots = middle_scratch[0], middle_scratch[1], middle_scratch[15]
    sem_tokens, sem_qkv, sem_proj = sem[0:4], sem[4:10], sem[10:16]
    sem_middle = sem[16:]
    me, rank = lax.axis_index("ctx"), lax.axis_index("tensor")
    mine = lax.axis_index("dp")
    mate = rank + 1 - 2 * lax.rem(rank, 2)
    peers = peers_of("ctx", blocks)
    piece = qkv.shape[1]
    rows, model = tokens.shape
    width = q_ref.shape[1]
    count = rows // 2 // PIECES

    def span(index):
        return pl.ds(pl.multiple_of((lax.rem(rank, 2) * PIECES + index) * count, count), count)

    greet_line(size, [peers, pair_group(data)])
    across = []
    for index in range(PIECES):
        for step, (_, where) in enumerate(peers):
            across.append(
                remote(
                    tokens.at[span(index)],
                    wide_tokens.at[me, span(index)],
                    sem_tokens[0].at[step, index],
                    sem_tokens[1].at[step, index],
                    where,
                )
            )
            across[-1].start()
    place_qkv = lambda index: wide_qkv.at[:, part_rows(index, piece)]
    place_proj = lambda index: wide_proj.at[index]
    place_up = lambda index: wide_up.at[part_rows(index, piece)]
    place_down = lambda index: wide_down.at[part_rows(index, piece)]
    copies = gather_start(data, qkv, place_qkv, sem_qkv)
    projs = gather_start(data, proj, place_proj, sem_proj)
    ups = gather_start(data, up, place_up, sem_middle[12:18])
    downs = gather_start(data, down, place_down, sem_middle[18:24])
    wide_qkv[:, part_rows(mine, piece)] = qkv[...]
    wide_proj[mine] = proj[...]
    wide_tokens[me] = tokens[...]
    wide_up[part_rows(mine, piece)] = up[...]
    wide_down[part_rows(mine, piece)] = down[...]
    for index, vector in enumerate(given):
        fixed[index : index + 1, : vector.shape[0]] = vector[...].reshape(1, -1)
    passed = []

    def forward_piece(index):
        for step in range(len(peers)):
            origin = lax.rem(me + blocks - step - 1, blocks)
            across[index * len(peers) + step].wait_recv()
            place = wide_tokens.at[origin, span(index)]
            passed.append(
                remote(place, place, sem_tokens[2].at[step, index], sem_tokens[3].at[step, index], {"tensor": mate})
            )
            passed[-1].start()

    for index in range(PIECES - 1):
        forward_piece(index)
    wait_all(gather_pass(data, copies, place_qkv, sem_qkv))
    forward_piece(PIECES - 1)
    block = math.gcd(rows // 2, ROW_BLOCK)

    def project(origin, step):
        there = part_rows(step, block)
        here = pl.ds(pl.multiple_of(origin * rows + step * block, block), block)
        found = wide_tokens[origin, there]
        k_ref[here] = matmul(found, wide_qkv[1]).astype(BF16)
        v_ref[here] = (matmul(found, wide_qkv[2]) + fixed[8:9, :width]).astype(BF16)

    @pl.loop(0, rows // block)
    def _(step):
        here = part_rows(step, block)
        q_ref[here] = (matmul(tokens[here], wide_qkv[0]) + fixed[7:8, :width]).astype(BF16)
        project(me, step)

    for slot, index in enumerate((1, 2, 0)):
        flat_ref[:, slot * width : (slot + 1) * width] = wide_qkv[index]
    wait_all(gather_pass(data, projs, place_proj, sem_proj))
    column = wide_proj.shape[2]
    for index in range(data):
        proj_ref[:, index * column : (index + 1) * column] = wide_proj[index]
    for copy in across:
        copy.wait_send()
    wait_all(passed)

    @pl.loop(0, (blocks - 1) * (rows // block))
    def _(step):
        other = lax.rem(me + 1 + lax.div(step, rows // block), blocks)
        project(other, lax.rem(step, rows // block))

    length = length_ref[0]
    keys = k_ref.shape[0]
    hidden_keys = lax.broadcasted_iota(jnp.int32, (block, keys), 1) >= length
    chunks, chunk = part.shape[1:3]
    group = block // chunk

    @pl.loop(0, rows // block)
    def _(step):
        here = part_rows(step, block)
        for head in range(width // HD):
            lanes = slice(head * HD, (head + 1) * HD)
            scores = matmul_last(q_ref[here, lanes], k_ref[:, lanes]) * score_scale
            scores = jnp.where(hidden_keys, NEGATIVE, scores)
            top = jnp.max(scores, axis=-1, keepdims=True)
            weights = jnp.exp(scores - top)
            total = jnp.sum(weights, axis=-1, keepdims=True)
            attended = matmul(weights.astype(BF16), v_ref[:, lanes]) / total
            out_ref[here, lanes] = attended
            low_ref[here, lanes] = attended.astype(BF16)
            log_ref[here, head : head + 1] = top + jnp.log(total)
        flow, begin = lax.div(step * group, chunks), lax.rem(step * group, chunks)
        result = matmul(low_ref[here], proj_ref[...]).astype(BF16)
        part[flow, pl.ds(begin, group)] = result.reshape(group, chunk, model)
        line_start_block(size, part, slots, sem_middle[0:4], flow, begin, group)

    passing = gather_pass(data, ups, place_up, sem_middle[12:18])
    passing += gather_pass(data, downs, place_down, sem_middle[18:24])
    middle_steps(sizes, passing, part, tokens, cotangent, fixed, up, *middle_outs, *middle_scratch, *sem_middle)


def near_start(size, grads, chip, sem):
    _, partner, _ = pair_roles(size)
    piece = chip.shape[1]
    copies = [
        remote(
            grads.at[part_rows(2 * index + lax.rem(partner, 2), piece)],
            chip.at[index],
            sem[0].at[index],
            sem[1].at[index],
            {"dp": partner},
        )
        for index in range(size // 2)
    ]
    for copy in copies:
        copy.start()
    return copies


def far_start(size, copies, grads, chip, merged, slots, sem):
    me, _, far = pair_roles(size)
    piece = chip.shape[1]
    wait_all(copies)
    for index in range(size // 2):
        own = grads[part_rows(2 * index + lax.rem(me, 2), piece)]
        merged[index] = (own.astype(F32) + chip[index].astype(F32)).astype(BF16)
    moving = [
        remote(
            merged.at[lax.div(to, 2)], slots.at[lax.div(me, 2)], sem[2].at[step], sem[3].at[step], {"dp": to}
        )
        for step, (to, _) in enumerate(far)
    ]
    for copy in moving:
        copy.start()
    slots[lax.div(me, 2)] = merged[lax.div(me, 2)]
    return moving


def blocks_start(sizes, value, blocks, sem):
    me = lax.axis_index("ctx")
    blocks[me] = value
    return send_all(
        lambda other: (blocks.at[me], blocks.at[me]), peers_of("ctx", sizes["ctx"]), sem[0], sem[1]
    )


def middle_steps(
    sizes, passing, part, tokens, cotangent, fixed, up,
    attn_low, attn_ref, output_ref, vector_ref, block_up, block_down,
    wide_up, wide_down, low, normed_ref, inverse_ref, out_ref, pre, hidden,
    part_two, back_ref, second_low, d_pre, part_three, grads_up, grads_down,
    slots, sums, slots_two, sums_two, slots_three, sums_three,
    chip_a, chip_b, merged_a, merged_b, far_a, far_b, *sem
):
    size, data = sizes["tensor"], sizes["dp"]
    mine = lax.axis_index("dp")
    piece = up.shape[0]
    chunks, chunk, model = part.shape[1:]
    group = math.gcd(chunks, GROUP)
    count = group * chunk
    steps = 2 * chunks // group
    line_one, line_two, line_three = sem[0:4], sem[4:8], sem[8:12]
    sem_up, sem_down = sem[12:18], sem[18:24]
    sem_a, sem_b = sem[24:28], sem[28:32]
    vector_ref[...] = jnp.zeros_like(vector_ref)

    def first_finish(flow, k, total):
        here = pl.ds(pl.multiple_of((flow * chunks + k) * chunk, chunk), chunk)
        first_sum = tokens[here].astype(F32) + total + fixed[0:1, :model]
        first_out, normed, inverse = layer_norm(first_sum, fixed[1:2, :model], fixed[2:3, :model])
        out_ref[k] = first_out
        normed_ref[k] = normed
        inverse_ref[k] = inverse
        return first_out.astype(BF16)

    line_run(size, part, slots, sums, low, line_one, first_finish)
    wait_all(passing)

    @pl.loop(0, steps)
    def _(step):
        flow, begin = block_of(step, group)
        here = pl.ds(pl.multiple_of(step * count, count), count)
        found = low[flow, pl.ds(begin, group)].reshape(count, model)
        value = matmul(found, wide_up[...]) + fixed[6:7, : pre.shape[1]]
        pre[here] = value
        hidden[here] = gelu_value(value).astype(BF16)
        result = matmul_last(hidden[here], wide_down[...]).astype(BF16)
        part_two[flow, pl.ds(begin, group)] = result.reshape(group, chunk, model)
        line_start_block(size, part_two, slots_two, line_two, flow, begin, group)

    def second_finish(flow, k, total):
        second_sum = out_ref[k] + total + fixed[3:4, :model]
        result, normed, inverse = layer_norm(second_sum, fixed[4:5, :model], fixed[5:6, :model])
        upstream = cotangent[flow, k].astype(F32)
        d_second = norm_back(upstream, normed, inverse, fixed[4:5, :model])
        output_ref[k] = result.astype(BF16)
        back_ref[k] = d_second
        add_row(vector_ref, 0, upstream)
        add_row(vector_ref, 1, upstream * normed)
        add_row(vector_ref, 2, d_second)
        return d_second.astype(BF16)

    def slope_work(step):
        @pl.when(step < 2 * chunks)
        def _():
            here = part_rows(step, chunk)
            pre[here] = gelu_slope(pre[here])

    line_run(size, part_two, slots_two, sums_two, second_low, line_two, second_finish, work=slope_work)

    @pl.loop(0, steps)
    def _(step):
        flow, begin = block_of(step, group)
        here = pl.ds(pl.multiple_of(step * count, count), count)
        found = second_low[flow, pl.ds(begin, group)].reshape(count, model)
        value = matmul(found, wide_down[...]) * pre[here]
        add_row(vector_ref, 6, value)
        d_pre[here] = value.astype(BF16)
        result = matmul_last(d_pre[here], wide_up[...]).astype(BF16)
        part_three[flow, pl.ds(begin, group)] = result.reshape(group, chunk, model)
        line_start_block(size, part_three, slots_three, line_three, flow, begin, group)

    def third_finish(flow, k, total):
        d_first = total + back_ref[k]
        normed = normed_ref[k]
        d_attn = norm_back(d_first, normed, inverse_ref[k], fixed[1:2, :model])
        attn_ref[k] = d_attn
        add_row(vector_ref, 3, d_first)
        add_row(vector_ref, 4, d_first * normed)
        add_row(vector_ref, 5, d_attn)
        return d_attn.astype(BF16)

    pieces = model // 128

    def grads_work(step):
        @pl.when(step < pieces)
        def _():
            columns = part_rows(step, 128)
            left = [
                second_low[block % 2, block // 2 * group : block // 2 * group + group, :, columns].reshape(count, 128)
                for block in range(steps)
            ]
            grads_down[columns] = matmul_first(jnp.concatenate(left, axis=0), hidden[...]).astype(BF16)

        @pl.when(jnp.logical_and(step >= pieces, step < 2 * pieces))
        def _():
            columns = part_rows(step - pieces, 128)
            left = [
                low[block % 2, block // 2 * group : block // 2 * group + group, :, columns].reshape(count, 128)
                for block in range(steps)
            ]
            grads_up[columns] = matmul_first(jnp.concatenate(left, axis=0), d_pre[...]).astype(BF16)

    near_a, near_b, moving_a, moving_b = [], [], [], []

    def near_down():
        near_b.extend(near_start(data, grads_down, chip_b, sem_b))

    def near_up():
        near_a.extend(near_start(data, grads_up, chip_a, sem_a))
        moving_b.extend(far_start(data, near_b, grads_down, chip_b, merged_b, far_b, sem_b))

    def far_up():
        moving_a.extend(far_start(data, near_a, grads_up, chip_a, merged_a, far_a, sem_a))

    between = [(pieces, near_down), (2 * pieces, near_up), (2 * pieces + LAG, far_up)]
    line_run(
        size, part_three, slots_three, sums_three, attn_low, line_three, third_finish, between, work=grads_work
    )
    wait_all(moving_b)
    block_down[...] = slot_sum(far_b, data // 2).astype(BF16)
    wait_all(moving_a)
    block_up[...] = slot_sum(far_a, data // 2).astype(BF16)


def back_kernel(
    sizes, score_scale, length_ref, q_ref, k_ref, v_ref, attended_ref, low_ref, log_ref,
    proj_ref, attn_low, tokens, vectors, flat, d_attn, block_a, block_b, mine,
    full, output_ref, owned, owned_a, owned_b, vector_ref,
    dk_ref, dv_ref, heads_ref, stack, grads, own_ref,
    part, slots, sums, keys, total_ref, chip, merged, far, blocks, blocks_a, blocks_b, slots_v, grid_v, *sem
):
    size, data = sizes["tensor"], sizes["dp"]
    rank, me = lax.axis_index("tensor"), lax.axis_index("ctx")
    chunks, chunk, model = part.shape[1:]
    group = math.gcd(chunks, GROUP)
    count = group * chunk
    steps = 2 * chunks // group
    wide = keys.shape[2]
    line, spread, sem_keys, sem_grads = sem[0:4], sem[4:6], sem[6:8], sem[8:12]
    sem_small, sem_grid, sem_a, sem_b, sem_last = sem[12:14], sem[14:16], sem[16:18], sem[18:20], sem[20:22]
    others = peers_of("ctx", sizes["ctx"])
    here_v, everyone = grid_peers(sizes)
    peers = peers_of("tensor", size)
    greet([peers, everyone])
    spread_start(size, mine, output_ref, spread)
    moving_a = blocks_start(sizes, block_a[...], blocks_a, sem_a)
    moving_b = blocks_start(sizes, block_b[...], blocks_b, sem_b)

    length = length_ref[0]
    rows, width = q_ref.shape
    total_keys = k_ref.shape[0]
    block = math.gcd(rows, ROW_BLOCK)
    hidden_keys = lax.broadcasted_iota(jnp.int32, (block, total_keys), 1) >= length
    dk_ref[...] = jnp.zeros_like(dk_ref)
    dv_ref[...] = jnp.zeros_like(dv_ref)
    own_ref[...] = vectors[...]
    stack[:, :, 2 * width :] = jnp.zeros((sizes["ctx"], rows, width), BF16)
    heads = width // HD
    turns = rows // block * heads
    relays = mine.shape[0] + SPREAD_LAG * (size - 1)

    @pl.loop(0, rows // block)
    def _(step):
        here = part_rows(step, block)
        heads_ref[here] = matmul_last(attn_low[here], proj_ref[...]).astype(BF16)
        for head in range(heads):
            lanes = slice(head * HD, (head + 1) * HD)
            q, k, v, d_heads = q_ref[here, lanes], k_ref[:, lanes], v_ref[:, lanes], heads_ref[here, lanes]
            delta = jnp.sum(d_heads.astype(F32) * attended_ref[here, lanes], axis=-1, keepdims=True)
            scores = matmul_last(q, k) * score_scale
            scores = jnp.where(hidden_keys, NEGATIVE, scores)
            probs = jnp.exp(scores - log_ref[here, head : head + 1])
            d_scores = (probs * (matmul_last(d_heads, v) - delta)).astype(BF16)
            dv_ref[:, lanes] += matmul_first(probs.astype(BF16), d_heads)
            dk_ref[:, lanes] += matmul_first(d_scores, q) * score_scale
            d_query = matmul(d_scores, k) * score_scale
            own_ref[7:8, lanes] += jnp.sum(d_query, axis=0, keepdims=True)
            stack[me, here, 2 * width + head * HD : 2 * width + (head + 1) * HD] = d_query.astype(BF16)
            turn = step * heads + head
            spread_steps(size, mine, output_ref, spread, turn * relays // turns, (turn + 1) * relays // turns)

    own_ref[7:8, width : 2 * width] = jnp.sum(dv_ref[...], axis=0, keepdims=True)
    stack[:, :, :width] = dk_ref[...].astype(BF16).reshape(sizes["ctx"], rows, width)
    stack[:, :, width : 2 * width] = dv_ref[...].astype(BF16).reshape(sizes["ctx"], rows, width)

    def span(step):
        flow, begin = step % 2, step // 2 * group
        return slice((flow * chunks + begin) * chunk, (flow * chunks + begin) * chunk + count)

    moving_keys = [
        [
            remote(
                stack.at[other, span(step), 0:wide],
                keys.at[me, span(step)],
                sem_keys[0].at[index, step],
                sem_keys[1].at[index, step],
                where,
            )
            for index, (other, where) in enumerate(others)
        ]
        for step in range(steps)
    ]
    for copies in moving_keys:
        for copy in copies:
            copy.start()
    small = send_all(lambda other: (own_ref, slots_v.at[rank]), peers, sem_small[0], sem_small[1])
    slots_v[rank] = own_ref[...]

    @pl.loop(0, model // 128)
    def _(index):
        columns = part_rows(index, 128)
        every = stack[...].reshape(total_keys, 3 * width)
        grads[columns, : 3 * width] = matmul_first(tokens[:, columns], every).astype(BF16)
        grads[columns, 3 * width :] = matmul_first(attn_low[:, columns], low_ref[...]).astype(BF16)

    near = near_start(data, grads, chip, sem_grads)
    state = {}

    def send_group(step):
        flow, begin = step % 2, step // 2 * group
        there = span(step)
        keys[me, there] = stack[me, there, 0:wide]
        for copy in moving_keys[step]:
            copy.wait_recv()
        total = keys[0, there].astype(F32)
        for index in range(1, sizes["ctx"]):
            total = total + keys[index, there].astype(F32)
        total_ref[there, 0:wide] = total.astype(BF16)
        total_ref[there, wide:] = stack[me, there, wide:]
        result = matmul_last(total_ref[there], flat[...]).astype(BF16)
        part[flow, begin : begin + group] = result.reshape(group, chunk, model)
        line_start_block(size, part, slots, line, flow, begin, group)

    def go_far():
        state["far"] = far_start(data, near, grads, chip, merged, far, sem_grads)
        wait_all(small)
        own = own_ref[...]
        row_ids = lax.broadcasted_iota(jnp.int32, own.shape, 0)
        grid_v[here_v] = jnp.where(row_ids < 6, slot_sum(slots_v, size), own)
        state["small"] = send_all(
            lambda other: (grid_v.at[here_v], grid_v.at[here_v]), everyone, sem_grid[0], sem_grid[1]
        )

    def go_across():
        wait_all(state["far"])
        value = slot_sum(far, data // 2).astype(BF16)
        state["across"] = blocks_start(sizes, value, blocks, sem_last)

    def finish(flow, k, total):
        return (total + d_attn[k]).astype(BF16)

    for step in range(2):
        send_group(step)
    between = [(1, go_far)]
    between += [(LAG + 2 * step - 3, functools.partial(send_group, step)) for step in range(2, steps)]
    between += [(max(LAG * size, LAG + 2 * steps), go_across)]
    line_run(size, part, slots, sums, full, line, finish, between)
    spread_end(size, mine, output_ref, spread)
    for copies in moving_keys:
        for copy in copies:
            copy.wait_send()
    wait_all(state["small"])
    vector_ref[...] = slot_sum(grid_v, data * sizes["ctx"])
    wait_all(moving_a)
    owned_a[...] = slot_sum(blocks_a, sizes["ctx"])
    wait_all(moving_b)
    owned_b[...] = slot_sum(blocks_b, sizes["ctx"])
    wait_all(state["across"])
    owned[...] = slot_sum(blocks, sizes["ctx"])


def unpack_kernel(
    full, output, owned, owned_a, owned_b, sums,
    output_ref, tokens_ref, qkv_ref, proj_ref, up_ref, down_ref, query_ref, value_ref, *rows
):
    width = qkv_ref.shape[2]
    output_ref[...] = output[...]
    tokens_ref[...] = full[...].astype(F32)
    for index, slot in enumerate((2, 0, 1)):
        qkv_ref[index] = owned[:, slot * width : (slot + 1) * width]
    proj_ref[...] = owned[:, 3 * width :].T
    up_ref[...] = owned_a[...]
    down_ref[...] = owned_b[...]
    query_ref[...] = sums[7, :width]
    value_ref[...] = sums[7, width : 2 * width]
    for index, row in enumerate(rows):
        row[...] = sums[index, : row.shape[0]]


def local_call(kernel, outs, scratch, args, name, scalars=1):
    return pl.pallas_call(
        kernel,
        out_shape=outs,
        in_specs=[pl.BlockSpec(memory_space=pltpu.SMEM)] * scalars + [VMEM_SPEC] * (len(args) - scalars),
        out_specs=[VMEM_SPEC] * len(outs),
        scratch_shapes=scratch,
        compiler_params=pltpu.CompilerParams(vmem_limit_bytes=60 * 2**20),
        name=name,
    )(*args)


def per_device(
    sizes,
    tokens,
    lengths,
    cotangent,
    qkv_weight,
    query_bias,
    value_bias,
    proj_weight,
    proj_bias,
    first_gain,
    first_shift,
    up_weight,
    up_bias,
    down_weight,
    down_bias,
    second_gain,
    second_shift,
):
    data, blocks, ranks = sizes["dp"], sizes["ctx"], sizes["tensor"]
    rows_in = tokens[0]
    row_count, model = rows_in.shape
    half = row_count // 2
    chunk = math.gcd(half, CHUNK)
    chunks = half // chunk
    piece, width = qkv_weight.shape[1:]
    up_width = up_weight.shape[1]
    keys = blocks * row_count
    score_scale = 1.0 / math.sqrt(HD)
    split = (2, chunks, chunk, model)
    flow = pltpu.VMEM(split, BF16)
    line = line_sems(chunks, 4)
    local = shaped(split[1:], F32)
    held = pltpu.VMEM(split[1:], F32)
    steps = 2 * chunks // math.gcd(chunks, GROUP)
    vector_width = max(model, up_width, 2 * width)
    given = (
        proj_bias, first_gain, first_shift, down_bias, second_gain, second_shift, up_bias, query_bias, value_bias
    )

    up_shape = (model, up_width)
    pair_slots = pltpu.VMEM((data // 2, model // data, up_width), BF16)
    pair_moves = sems(data // 2) + sems(max(1, data // 2 - 1))
    (
        queries, key_rows, value_rows, attended, attended_low, log_total, flat_proj, flat_qkv, wide_tokens,
        attn_low, d_attn, output_part, vectors, block_up, block_down,
    ) = call(
        functools.partial(front_kernel, sizes, score_scale, len(given)),
        [
            shaped((row_count, width), BF16),
            shaped((keys, width), BF16),
            shaped((keys, width), BF16),
            shaped((row_count, width), F32),
            shaped((row_count, width), BF16),
            shaped((row_count, width // HD), F32),
            shaped((width, model), BF16),
            shaped((model, 3 * width), BF16),
            shaped((blocks, row_count, model), BF16),
            shaped(split, BF16),
            local,
            shaped(split[1:], BF16),
            shaped((8, vector_width), F32),
            shaped((model // data, up_width), BF16),
            shaped((model // data, up_width), BF16),
        ],
        [
            pltpu.VMEM((3, model, width), BF16),
            pltpu.VMEM((data,) + proj_weight.shape, BF16),
            pltpu.VMEM((16, vector_width), F32),
            flow,
        ]
        + [
            pltpu.VMEM(up_shape, BF16),
            pltpu.VMEM(up_shape, BF16),
            flow,
            held,
            pltpu.VMEM((chunks, chunk, 1), F32),
            held,
            pltpu.VMEM((row_count, up_width), F32),
            pltpu.VMEM((row_count, up_width), BF16),
            flow,
            held,
            flow,
            pltpu.VMEM((row_count, up_width), BF16),
            flow,
            pltpu.VMEM(up_shape, BF16),
            pltpu.VMEM(up_shape, BF16),
        ]
        + [flow] * 6
        + [pair_slots] * 6
        + [DMA((max(1, blocks - 1), PIECES))] * 4
        + pair_sems(data) * 2
        + line * 3
        + pair_sems(data) * 2
        + pair_moves * 2,
        1,
        (lengths, rows_in, qkv_weight, proj_weight, cotangent[0].reshape(split), up_weight, down_weight.T) + given,
        "forward_and_hidden",
        scalars=1,
    )
    wide_tokens = wide_tokens.reshape(keys, model)

    own_shape = (model // data, 4 * width)
    last_pair = pltpu.VMEM((data // 2,) + own_shape, BF16)
    grad_tokens, output, own_last, own_up, own_down, sums = call(
        functools.partial(back_kernel, sizes, score_scale),
        [
            shaped(split, BF16),
            shaped(split, BF16),
            shaped(own_shape, F32),
            shaped((model // data, up_width), F32),
            shaped((model // data, up_width), F32),
            shaped(vectors.shape, F32),
        ],
        [
            pltpu.VMEM((keys, width), F32),
            pltpu.VMEM((keys, width), F32),
            pltpu.VMEM((row_count, width), BF16),
            pltpu.VMEM((blocks, row_count, 3 * width), BF16),
            pltpu.VMEM((model, 4 * width), BF16),
            pltpu.VMEM(vectors.shape, F32),
        ]
        + [flow] * 3
        + [
            pltpu.VMEM((blocks, row_count, 2 * width), BF16),
            pltpu.VMEM((row_count, 3 * width), BF16),
        ]
        + [last_pair] * 3
        + [pltpu.VMEM((blocks,) + own_shape, BF16)]
        + [pltpu.VMEM((blocks, model // data, up_width), BF16)] * 2
        + [
            pltpu.VMEM((ranks,) + vectors.shape, F32),
            pltpu.VMEM((data * blocks,) + vectors.shape, F32),
        ]
        + line
        + line_sems(chunks, 2)
        + [DMA((max(1, blocks - 1), steps))] * 2
        + pair_moves
        + sems(ranks - 1)
        + sems(data * blocks - 1)
        + sems(blocks - 1) * 3,
        2,
        (
            lengths, queries, key_rows, value_rows, attended, attended_low, log_total,
            flat_proj, attn_low.reshape(row_count, model), wide_tokens, vectors,
            flat_qkv, d_attn, block_up, block_down, output_part,
        ),
        "attention_backward",
        scalars=1,
    )
    output, grad_tokens, own_qkv, own_proj, own_up, own_down, grad_query, grad_value, *rows = local_call(
        unpack_kernel,
        [
            shaped((row_count, model), BF16),
            shaped((row_count, model), F32),
            shaped((3, model // data, width), F32),
            shaped((width, model // data), F32),
            shaped(own_up.shape, F32),
            shaped(own_down.shape, F32),
            shaped((width,), F32),
            shaped((width,), F32),
        ]
        + [shaped((model,), F32)] * 6
        + [shaped((up_width,), F32)],
        [],
        (
            grad_tokens.reshape(row_count, model),
            output.reshape(row_count, model),
            own_last,
            own_up,
            own_down,
            sums,
        ),
        "unpack",
        scalars=0,
    )
    return (
        output[None],
        grad_tokens[None],
        own_qkv,
        grad_query,
        grad_value,
        own_proj,
        rows[5],
        rows[4],
        rows[3],
        own_up,
        rows[6],
        own_down.T,
        rows[2],
        rows[1],
        rows[0],
    )


def solution(mesh):
    placed = (
        P("dp", "ctx", None),
        P("dp"),
        P("dp", "ctx", None),
        P(None, "dp", "tensor"),
        P("tensor"),
        P("tensor"),
        P("tensor", "dp"),
        P(),
        P(),
        P(),
        P("dp", "tensor"),
        P("tensor"),
        P("tensor", "dp"),
        P(),
        P(),
        P(),
    )
    return jax.shard_map(
        functools.partial(per_device, dict(mesh.shape)),
        mesh=mesh,
        in_specs=placed,
        out_specs=(
            P("dp", "ctx", None),
            P("dp", "ctx", None),
            P(None, "dp", "tensor"),
            P("tensor"),
            P("tensor"),
            P("tensor", "dp"),
            P(),
            P(),
            P(),
            P("dp", "tensor"),
            P("tensor"),
            P("tensor", "dp"),
            P(),
            P(),
            P(),
        ),
        check_vma=False,
    )
```

```python
import functools
import math

import jax
import jax.numpy as jnp
from jax import lax
from jax.experimental import pallas as pl
from jax.experimental.pallas import tpu as pltpu
from jax.sharding import PartitionSpec as P

HD = 64


EPSILON = 1e-05
NEGATIVE = -1e30
ROOT_HALF = 0.7071067811865476
ROOT_TWO_PI = 2.5066282746310002
MESH = pl.DeviceIdType.MESH
BF16 = jnp.bfloat16
F32 = jnp.float32
VMEM_SPEC = pl.BlockSpec(memory_space=pltpu.VMEM)
DMA = pltpu.SemaphoreType.DMA


def layer_norm(hidden_in, norm_gain, norm_shift):
    centred = hidden_in - jnp.mean(hidden_in, axis=-1, keepdims=True)
    inverse = lax.rsqrt(jnp.mean(centred * centred, axis=-1, keepdims=True) + EPSILON)
    normed = centred * inverse
    return (normed * norm_gain + norm_shift, normed, inverse)


def norm_back(upstream, normed, inverse, norm_gain):
    scaled = upstream * norm_gain
    return inverse * (
        scaled
        - jnp.mean(scaled, axis=-1, keepdims=True)
        - normed * jnp.mean(scaled * normed, axis=-1, keepdims=True)
    )


def gelu_value(pre_act):
    return 0.5 * pre_act * (1.0 + jax.scipy.special.erf(pre_act * ROOT_HALF))


def gelu_slope(pre_act):
    return (
        0.5 * (1.0 + jax.scipy.special.erf(pre_act * ROOT_HALF))
        + pre_act * jnp.exp(-0.5 * pre_act * pre_act) / ROOT_TWO_PI
    )


def peers_of(axis, size):
    me = lax.axis_index(axis)
    found = []
    for step in range(1, size):
        other = lax.rem(me + step, size)
        found.append((other, {axis: other}))
    return found


def grid_peers(sizes):
    count = sizes["dp"] * sizes["ctx"]
    me = lax.axis_index("dp") * sizes["ctx"] + lax.axis_index("ctx")
    found = []
    for step in range(1, count):
        other = lax.rem(me + step, count)
        found.append((other, {"dp": lax.div(other, sizes["ctx"]), "ctx": lax.rem(other, sizes["ctx"])}))
    return me, found


def greet(groups):
    barrier = pltpu.get_barrier_semaphore()
    total = 0
    for group in groups:
        for _, where in group:
            pl.semaphore_signal(barrier, inc=1, device_id=where, device_id_type=MESH)
            total += 1
    pl.semaphore_wait(barrier, total)


def send_all(pairs, peers, send_sem, recv_sem):
    copies = []
    for step, (other, where) in enumerate(peers):
        source, target = pairs(other)
        copies.append(
            pltpu.make_async_remote_copy(
                src_ref=source,
                dst_ref=target,
                send_sem=send_sem.at[step],
                recv_sem=recv_sem.at[step],
                device_id=where,
                device_id_type=MESH,
            )
        )
        copies[-1].start()
    return copies


def wait_all(copies):
    for copy in copies:
        copy.wait()


def slot_sum(slots, count):
    total = slots[0].astype(F32)
    for index in range(1, count):
        total = total + slots[index].astype(F32)
    return total


def sems(count):
    return [DMA((count,)), DMA((count,))]


def call(kernel, outs, scratch, collective_id, args, name, scalars=0):
    return pl.pallas_call(
        kernel,
        out_shape=outs,
        in_specs=[pl.BlockSpec(memory_space=pltpu.SMEM)] * scalars + [VMEM_SPEC] * (len(args) - scalars),
        out_specs=[VMEM_SPEC] * len(outs),
        scratch_shapes=scratch,
        compiler_params=pltpu.CompilerParams(
            collective_id=collective_id, has_side_effects=True, vmem_limit_bytes=62 * 2**20
        ),
        name=name,
    )(*args)


def shaped(shape, dtype):
    return jax.ShapeDtypeStruct(shape, dtype)


def pair_roles(size):
    me = lax.axis_index("dp")
    partner = me + 1 - 2 * lax.rem(me, 2)
    far = [(lax.rem(me + 2 * step, size), lax.rem(me + size - 2 * step, size)) for step in range(1, size // 2)]
    return me, partner, far


def pair_group(size):
    me, partner, far = pair_roles(size)
    return [(partner, {"dp": partner})] + [(to, {"dp": to}) for to, _ in far]


def remote(source, target, send, recv, where):
    return pltpu.make_async_remote_copy(
        src_ref=source, dst_ref=target, send_sem=send, recv_sem=recv, device_id=where, device_id_type=MESH
    )


def pair_sems(size):
    return sems(1) + sems(max(1, size // 2 - 1)) * 2


def gather_start(size, own_ref, place, sem):
    me, partner, far = pair_roles(size)
    near = remote(own_ref, place(me), sem[0].at[0], sem[1].at[0], {"dp": partner})
    wide = [
        remote(own_ref, place(me), sem[2].at[step], sem[3].at[step], {"dp": to})
        for step, (to, _) in enumerate(far)
    ]
    for copy in wide + [near]:
        copy.start()
    return near, wide


def gather_pass(size, copies, place, sem):
    me, partner, far = pair_roles(size)
    passed = []
    for step, (_, origin) in enumerate(far):
        copies[1][step].wait()
        passed.append(
            remote(place(origin), place(origin), sem[4].at[step], sem[5].at[step], {"dp": partner})
        )
        passed[-1].start()
    return [copies[0]] + passed


LAG = 4
CHUNK = 32


def line_roles(size):
    me = lax.axis_index("tensor")
    lower, upper = lax.rem(me + size - 1, size), lax.rem(me + 1, size)
    return [(me, lower, upper), (size - 1 - me, upper, lower)]


def greet_line(size, groups):
    me = lax.axis_index("tensor")
    barrier = pltpu.get_barrier_semaphore()

    @pl.when(me > 0)
    def _():
        pl.semaphore_signal(barrier, inc=1, device_id={"tensor": me - 1}, device_id_type=MESH)

    @pl.when(me < size - 1)
    def _():
        pl.semaphore_signal(barrier, inc=1, device_id={"tensor": me + 1}, device_id_type=MESH)

    total = 0
    for group in groups:
        for _, where in group:
            pl.semaphore_signal(barrier, inc=1, device_id=where, device_id_type=MESH)
            total += 1

    beside = jnp.where(me > 0, 1, 0) + jnp.where(me < size - 1, 1, 0)
    pl.semaphore_wait(barrier, total + beside)


def both(*conditions):
    return functools.reduce(jnp.logical_and, conditions)


def line_start(size, part, slots, sem):
    count = part.shape[1]
    for flow, (place, toward, _) in enumerate(line_roles(size)):

        @pl.when(place == size - 1)
        def _(flow=flow, toward=toward):
            @pl.loop(0, count)
            def _(k):
                remote(
                    part.at[flow, k], slots.at[flow, k], sem[0].at[flow, k], sem[1].at[flow, k], {"tensor": toward}
                ).start()


def line_start_block(size, part, slots, sem, flow, begin, count):
    me = lax.axis_index("tensor")
    lower, upper = lax.rem(me + size - 1, size), lax.rem(me + 1, size)
    place = jnp.where(flow == 0, me, size - 1 - me)
    toward = jnp.where(flow == 0, lower, upper)

    @pl.when(place == size - 1)
    def _():
        @pl.loop(0, count)
        def _(step):
            k = begin + step
            remote(
                part.at[flow, k], slots.at[flow, k], sem[0].at[flow, k], sem[1].at[flow, k], {"tensor": toward}
            ).start()


def line_run(size, part, slots, sums, full, sem, finish, between=(), work=None):
    count = part.shape[1]
    roles = line_roles(size)

    def reduce_copy(flow, k, source):
        return remote(
            source.at[flow, k], slots.at[flow, k], sem[0].at[flow, k], sem[1].at[flow, k], {"tensor": roles[flow][1]}
        )

    def spread_copy(flow, k):
        return remote(
            full.at[flow, k], full.at[flow, k], sem[2].at[flow, k], sem[3].at[flow, k], {"tensor": roles[flow][2]}
        )

    def one_step(step):
        if work is not None:
            work(step)

        for flow, (place, _, _) in enumerate(roles):
            k = step - LAG * (size - 1 - place)
            inside = both(k >= 0, k < count)

            @pl.when(both(inside, place > 0, place < size - 1))
            def _(flow=flow, k=k):
                reduce_copy(flow, k, sums).wait_recv()
                sums[flow, k] = (slots[flow, k].astype(F32) + part[flow, k].astype(F32)).astype(BF16)
                reduce_copy(flow, k, sums).start()

            @pl.when(both(inside, place == 0))
            def _(flow=flow, k=k):
                reduce_copy(flow, k, sums).wait_recv()
                full[flow, k] = finish(flow, k, slots[flow, k].astype(F32) + part[flow, k].astype(F32))
                spread_copy(flow, k).start()

        for flow, (place, _, _) in enumerate(roles):
            k = step - LAG * (size - 1) - LAG * place
            inside = both(k >= 0, k < count, place > 0)

            @pl.when(inside)
            def _(flow=flow, k=k):
                spread_copy(flow, k).wait_recv()

            @pl.when(both(inside, place < size - 1))
            def _(flow=flow, k=k):
                spread_copy(flow, k).start()

    begun, last = 0, count + 2 * LAG * (size - 1)
    for stop, action in tuple(between) + ((last, None),):
        stop = min(stop, last)
        pl.loop(begun, stop)(one_step)
        begun = stop
        if action is not None:
            action()

    for flow, (place, _, _) in enumerate(roles):

        @pl.when(place > 0)
        def _(flow=flow):
            @pl.loop(0, count)
            def _(k):
                reduce_copy(flow, k, sums).wait_send()

        @pl.when(place < size - 1)
        def _(flow=flow):
            @pl.loop(0, count)
            def _(k):
                spread_copy(flow, k).wait_send()


def spread_start(size, mine, full, sem):
    for flow, (place, _, away) in enumerate(line_roles(size)):

        @pl.when(place == 0)
        def _(flow=flow, away=away):
            @pl.loop(0, mine.shape[0])
            def _(k):
                remote(
                    mine.at[k], full.at[flow, k], sem[0].at[flow, k], sem[1].at[flow, k], {"tensor": away}
                ).start()
                full[flow, k] = mine[k]


def spread_copy(size, flow, k, full, sem):
    toward = line_roles(size)[flow][2]
    return remote(full.at[flow, k], full.at[flow, k], sem[0].at[flow, k], sem[1].at[flow, k], {"tensor": toward})


def spread_steps(size, mine, full, sem, begin, end):
    count = mine.shape[0]

    @pl.loop(begin, end)
    def _(step):
        for flow, (place, _, _) in enumerate(line_roles(size)):
            k = step - SPREAD_LAG * place
            inside = both(k >= 0, k < count, place > 0)

            @pl.when(inside)
            def _(flow=flow, k=k):
                spread_copy(size, flow, k, full, sem).wait_recv()

            @pl.when(both(inside, place < size - 1))
            def _(flow=flow, k=k):
                spread_copy(size, flow, k, full, sem).start()


def spread_end(size, mine, full, sem):
    for flow, (place, _, _) in enumerate(line_roles(size)):

        @pl.when(place < size - 1)
        def _(flow=flow):
            @pl.loop(0, mine.shape[0])
            def _(k):
                spread_copy(size, flow, k, full, sem).wait_send()


def line_sems(count, kinds):
    return [DMA((2, count))] * kinds


def add_row(vector_ref, index, value):
    vector_ref[index : index + 1] += jnp.sum(value, axis=0, keepdims=True)


CONTRACT_LAST = (((1,), (1,)), ((), ()))
CONTRACT_FIRST = (((0,), (0,)), ((), ()))


PIECES = 4
GROUP = 4
ROW_BLOCK = 256
SPREAD_LAG = 4


def matmul(left, right):
    return jnp.dot(left, right, preferred_element_type=F32)


def matmul_last(left, right):
    return lax.dot_general(left, right, CONTRACT_LAST, preferred_element_type=F32)


def matmul_first(left, right):
    return lax.dot_general(left, right, CONTRACT_FIRST, preferred_element_type=F32)


def part_rows(index, count):
    return pl.ds(pl.multiple_of(index * count, count), count)


def block_of(step, group):
    return lax.rem(step, 2), lax.div(step, 2) * group


def front_kernel(
    sizes, score_scale, given_count, length_ref, tokens, qkv, proj, cotangent, up, down, *refs
):
    data, blocks, size = sizes["dp"], sizes["ctx"], sizes["tensor"]
    given, refs = refs[:given_count], refs[given_count:]
    q_ref, k_ref, v_ref, out_ref, low_ref, log_ref, proj_ref, flat_ref, wide_tokens = refs[:9]
    middle_outs, refs = refs[9:15], refs[15:]
    wide_qkv, wide_proj, fixed, part = refs[:4]
    middle_scratch, sem = refs[4:31], refs[31:]
    wide_up, wide_down, slots = middle_scratch[0], middle_scratch[1], middle_scratch[15]
    sem_tokens, sem_qkv, sem_proj = sem[0:4], sem[4:10], sem[10:16]
    sem_middle = sem[16:]
    me, rank = lax.axis_index("ctx"), lax.axis_index("tensor")
    mine = lax.axis_index("dp")
    mate = rank + 1 - 2 * lax.rem(rank, 2)
    peers = peers_of("ctx", blocks)
    piece = qkv.shape[1]
    rows, model = tokens.shape
    width = q_ref.shape[1]
    count = rows // 2 // PIECES

    def span(index):
        return pl.ds(pl.multiple_of((lax.rem(rank, 2) * PIECES + index) * count, count), count)

    greet_line(size, [peers, pair_group(data)])
    across = []
    for index in range(PIECES):
        for step, (_, where) in enumerate(peers):
            across.append(
                remote(
                    tokens.at[span(index)],
                    wide_tokens.at[me, span(index)],
                    sem_tokens[0].at[step, index],
                    sem_tokens[1].at[step, index],
                    where,
                )
            )
            across[-1].start()
    place_qkv = lambda index: wide_qkv.at[:, part_rows(index, piece)]
    place_proj = lambda index: wide_proj.at[index]
    place_up = lambda index: wide_up.at[part_rows(index, piece)]
    place_down = lambda index: wide_down.at[part_rows(index, piece)]
    copies = gather_start(data, qkv, place_qkv, sem_qkv)
    projs = gather_start(data, proj, place_proj, sem_proj)
    ups = gather_start(data, up, place_up, sem_middle[12:18])
    downs = gather_start(data, down, place_down, sem_middle[18:24])
    wide_qkv[:, part_rows(mine, piece)] = qkv[...]
    wide_proj[mine] = proj[...]
    wide_tokens[me] = tokens[...]
    wide_up[part_rows(mine, piece)] = up[...]
    wide_down[part_rows(mine, piece)] = down[...]
    for index, vector in enumerate(given):
        fixed[index : index + 1, : vector.shape[0]] = vector[...].reshape(1, -1)
    passed = []

    def forward_piece(index):
        for step in range(len(peers)):
            origin = lax.rem(me + blocks - step - 1, blocks)
            across[index * len(peers) + step].wait_recv()
            place = wide_tokens.at[origin, span(index)]
            passed.append(
                remote(place, place, sem_tokens[2].at[step, index], sem_tokens[3].at[step, index], {"tensor": mate})
            )
            passed[-1].start()

    for index in range(PIECES - 1):
        forward_piece(index)
    wait_all(gather_pass(data, copies, place_qkv, sem_qkv))
    forward_piece(PIECES - 1)
    block = math.gcd(rows // 2, ROW_BLOCK)

    def project(origin, step):
        there = part_rows(step, block)
        here = pl.ds(pl.multiple_of(origin * rows + step * block, block), block)
        found = wide_tokens[origin, there]
        k_ref[here] = matmul(found, wide_qkv[1]).astype(BF16)
        v_ref[here] = (matmul(found, wide_qkv[2]) + fixed[8:9, :width]).astype(BF16)

    @pl.loop(0, rows // block)
    def _(step):
        here = part_rows(step, block)
        q_ref[here] = (matmul(tokens[here], wide_qkv[0]) + fixed[7:8, :width]).astype(BF16)
        project(me, step)

    for slot, index in enumerate((1, 2, 0)):
        flat_ref[:, slot * width : (slot + 1) * width] = wide_qkv[index]
    wait_all(gather_pass(data, projs, place_proj, sem_proj))
    column = wide_proj.shape[2]
    for index in range(data):
        proj_ref[:, index * column : (index + 1) * column] = wide_proj[index]
    for copy in across:
        copy.wait_send()
    wait_all(passed)

    @pl.loop(0, (blocks - 1) * (rows // block))
    def _(step):
        other = lax.rem(me + 1 + lax.div(step, rows // block), blocks)
        project(other, lax.rem(step, rows // block))

    length = length_ref[0]
    keys = k_ref.shape[0]
    hidden_keys = lax.broadcasted_iota(jnp.int32, (block, keys), 1) >= length
    chunks, chunk = part.shape[1:3]
    group = block // chunk

    @pl.loop(0, rows // block)
    def _(step):
        here = part_rows(step, block)
        for head in range(width // HD):
            lanes = slice(head * HD, (head + 1) * HD)
            scores = matmul_last(q_ref[here, lanes], k_ref[:, lanes]) * score_scale
            scores = jnp.where(hidden_keys, NEGATIVE, scores)
            top = jnp.max(scores, axis=-1, keepdims=True)
            weights = jnp.exp(scores - top)
            total = jnp.sum(weights, axis=-1, keepdims=True)
            attended = matmul(weights.astype(BF16), v_ref[:, lanes]) / total
            out_ref[here, lanes] = attended
            low_ref[here, lanes] = attended.astype(BF16)
            log_ref[here, head : head + 1] = top + jnp.log(total)
        flow, begin = lax.div(step * group, chunks), lax.rem(step * group, chunks)
        result = matmul(low_ref[here], proj_ref[...]).astype(BF16)
        part[flow, pl.ds(begin, group)] = result.reshape(group, chunk, model)
        line_start_block(size, part, slots, sem_middle[0:4], flow, begin, group)

    passing = gather_pass(data, ups, place_up, sem_middle[12:18])
    passing += gather_pass(data, downs, place_down, sem_middle[18:24])
    middle_steps(sizes, passing, part, tokens, cotangent, fixed, up, *middle_outs, *middle_scratch, *sem_middle)


def near_start(size, grads, chip, sem):
    _, partner, _ = pair_roles(size)
    piece = chip.shape[1]
    copies = [
        remote(
            grads.at[part_rows(2 * index + lax.rem(partner, 2), piece)],
            chip.at[index],
            sem[0].at[index],
            sem[1].at[index],
            {"dp": partner},
        )
        for index in range(size // 2)
    ]
    for copy in copies:
        copy.start()
    return copies


def far_start(size, copies, grads, chip, merged, slots, sem):
    me, _, far = pair_roles(size)
    piece = chip.shape[1]
    wait_all(copies)
    for index in range(size // 2):
        own = grads[part_rows(2 * index + lax.rem(me, 2), piece)]
        merged[index] = (own.astype(F32) + chip[index].astype(F32)).astype(BF16)
    moving = [
        remote(
            merged.at[lax.div(to, 2)], slots.at[lax.div(me, 2)], sem[2].at[step], sem[3].at[step], {"dp": to}
        )
        for step, (to, _) in enumerate(far)
    ]
    for copy in moving:
        copy.start()
    slots[lax.div(me, 2)] = merged[lax.div(me, 2)]
    return moving


def blocks_start(sizes, value, blocks, sem):
    me = lax.axis_index("ctx")
    blocks[me] = value
    return send_all(
        lambda other: (blocks.at[me], blocks.at[me]), peers_of("ctx", sizes["ctx"]), sem[0], sem[1]
    )


def middle_steps(
    sizes, passing, part, tokens, cotangent, fixed, up,
    attn_low, attn_ref, output_ref, vector_ref, block_up, block_down,
    wide_up, wide_down, low, normed_ref, inverse_ref, out_ref, pre, hidden,
    part_two, back_ref, second_low, d_pre, part_three, grads_up, grads_down,
    slots, sums, slots_two, sums_two, slots_three, sums_three,
    chip_a, chip_b, merged_a, merged_b, far_a, far_b, *sem
):
    size, data = sizes["tensor"], sizes["dp"]
    mine = lax.axis_index("dp")
    piece = up.shape[0]
    chunks, chunk, model = part.shape[1:]
    group = math.gcd(chunks, GROUP)
    count = group * chunk
    steps = 2 * chunks // group
    line_one, line_two, line_three = sem[0:4], sem[4:8], sem[8:12]
    sem_up, sem_down = sem[12:18], sem[18:24]
    sem_a, sem_b = sem[24:28], sem[28:32]
    vector_ref[...] = jnp.zeros_like(vector_ref)

    def first_finish(flow, k, total):
        here = pl.ds(pl.multiple_of((flow * chunks + k) * chunk, chunk), chunk)
        first_sum = tokens[here].astype(F32) + total + fixed[0:1, :model]
        first_out, normed, inverse = layer_norm(first_sum, fixed[1:2, :model], fixed[2:3, :model])
        out_ref[k] = first_out
        normed_ref[k] = normed
        inverse_ref[k] = inverse
        return first_out.astype(BF16)

    line_run(size, part, slots, sums, low, line_one, first_finish)
    wait_all(passing)

    @pl.loop(0, steps)
    def _(step):
        flow, begin = block_of(step, group)
        here = pl.ds(pl.multiple_of(step * count, count), count)
        found = low[flow, pl.ds(begin, group)].reshape(count, model)
        value = matmul(found, wide_up[...]) + fixed[6:7, : pre.shape[1]]
        pre[here] = value
        hidden[here] = gelu_value(value).astype(BF16)
        result = matmul_last(hidden[here], wide_down[...]).astype(BF16)
        part_two[flow, pl.ds(begin, group)] = result.reshape(group, chunk, model)
        line_start_block(size, part_two, slots_two, line_two, flow, begin, group)

    def second_finish(flow, k, total):
        second_sum = out_ref[k] + total + fixed[3:4, :model]
        result, normed, inverse = layer_norm(second_sum, fixed[4:5, :model], fixed[5:6, :model])
        upstream = cotangent[flow, k].astype(F32)
        d_second = norm_back(upstream, normed, inverse, fixed[4:5, :model])
        output_ref[k] = result.astype(BF16)
        back_ref[k] = d_second
        add_row(vector_ref, 0, upstream)
        add_row(vector_ref, 1, upstream * normed)
        add_row(vector_ref, 2, d_second)
        return d_second.astype(BF16)

    def slope_work(step):
        @pl.when(step < 2 * chunks)
        def _():
            here = part_rows(step, chunk)
            pre[here] = gelu_slope(pre[here])

    line_run(size, part_two, slots_two, sums_two, second_low, line_two, second_finish, work=slope_work)

    @pl.loop(0, steps)
    def _(step):
        flow, begin = block_of(step, group)
        here = pl.ds(pl.multiple_of(step * count, count), count)
        found = second_low[flow, pl.ds(begin, group)].reshape(count, model)
        value = matmul(found, wide_down[...]) * pre[here]
        add_row(vector_ref, 6, value)
        d_pre[here] = value.astype(BF16)
        result = matmul_last(d_pre[here], wide_up[...]).astype(BF16)
        part_three[flow, pl.ds(begin, group)] = result.reshape(group, chunk, model)
        line_start_block(size, part_three, slots_three, line_three, flow, begin, group)

    def third_finish(flow, k, total):
        d_first = total + back_ref[k]
        normed = normed_ref[k]
        d_attn = norm_back(d_first, normed, inverse_ref[k], fixed[1:2, :model])
        attn_ref[k] = d_attn
        add_row(vector_ref, 3, d_first)
        add_row(vector_ref, 4, d_first * normed)
        add_row(vector_ref, 5, d_attn)
        return d_attn.astype(BF16)

    pieces = model // 128

    def grads_work(step):
        @pl.when(step < pieces)
        def _():
            columns = part_rows(step, 128)
            left = [
                second_low[block % 2, block // 2 * group : block // 2 * group + group, :, columns].reshape(count, 128)
                for block in range(steps)
            ]
            grads_down[columns] = matmul_first(jnp.concatenate(left, axis=0), hidden[...]).astype(BF16)

        @pl.when(jnp.logical_and(step >= pieces, step < 2 * pieces))
        def _():
            columns = part_rows(step - pieces, 128)
            left = [
                low[block % 2, block // 2 * group : block // 2 * group + group, :, columns].reshape(count, 128)
                for block in range(steps)
            ]
            grads_up[columns] = matmul_first(jnp.concatenate(left, axis=0), d_pre[...]).astype(BF16)

    near_a, near_b, moving_a, moving_b = [], [], [], []

    def near_down():
        near_b.extend(near_start(data, grads_down, chip_b, sem_b))

    def near_up():
        near_a.extend(near_start(data, grads_up, chip_a, sem_a))
        moving_b.extend(far_start(data, near_b, grads_down, chip_b, merged_b, far_b, sem_b))

    def far_up():
        moving_a.extend(far_start(data, near_a, grads_up, chip_a, merged_a, far_a, sem_a))

    between = [(pieces, near_down), (2 * pieces, near_up), (2 * pieces + LAG, far_up)]
    line_run(
        size, part_three, slots_three, sums_three, attn_low, line_three, third_finish, between, work=grads_work
    )
    wait_all(moving_b)
    block_down[...] = slot_sum(far_b, data // 2).astype(BF16)
    wait_all(moving_a)
    block_up[...] = slot_sum(far_a, data // 2).astype(BF16)


def back_kernel(
    sizes, score_scale, length_ref, q_ref, k_ref, v_ref, attended_ref, low_ref, log_ref,
    proj_ref, attn_low, tokens, vectors, flat, d_attn, block_a, block_b, mine,
    full, output_ref, owned, owned_a, owned_b, vector_ref,
    dk_ref, dv_ref, heads_ref, stack, grads, own_ref,
    part, slots, sums, keys, total_ref, chip, merged, far, blocks, blocks_a, blocks_b, slots_v, grid_v, *sem
):
    size, data = sizes["tensor"], sizes["dp"]
    rank, me = lax.axis_index("tensor"), lax.axis_index("ctx")
    chunks, chunk, model = part.shape[1:]
    group = math.gcd(chunks, GROUP)
    count = group * chunk
    steps = 2 * chunks // group
    wide = keys.shape[2]
    line, spread, sem_keys, sem_grads = sem[0:4], sem[4:6], sem[6:8], sem[8:12]
    sem_small, sem_grid, sem_a, sem_b, sem_last = sem[12:14], sem[14:16], sem[16:18], sem[18:20], sem[20:22]
    others = peers_of("ctx", sizes["ctx"])
    here_v, everyone = grid_peers(sizes)
    peers = peers_of("tensor", size)
    greet([peers, everyone])
    spread_start(size, mine, output_ref, spread)
    moving_a = blocks_start(sizes, block_a[...], blocks_a, sem_a)
    moving_b = blocks_start(sizes, block_b[...], blocks_b, sem_b)

    length = length_ref[0]
    rows, width = q_ref.shape
    total_keys = k_ref.shape[0]
    block = math.gcd(rows, ROW_BLOCK)
    hidden_keys = lax.broadcasted_iota(jnp.int32, (block, total_keys), 1) >= length
    dk_ref[...] = jnp.zeros_like(dk_ref)
    dv_ref[...] = jnp.zeros_like(dv_ref)
    own_ref[...] = vectors[...]
    stack[:, :, 2 * width :] = jnp.zeros((sizes["ctx"], rows, width), BF16)
    heads = width // HD
    turns = rows // block * heads
    relays_all = mine.shape[0] + SPREAD_LAG * (size - 1)
    relays_sent = mine.shape[0] + SPREAD_LAG * (size - 2)
    relays = relays_sent - 2

    @pl.loop(0, rows // block)
    def _(step):
        here = part_rows(step, block)
        heads_ref[here] = matmul_last(attn_low[here], proj_ref[...]).astype(BF16)
        for head in range(heads):
            lanes = slice(head * HD, (head + 1) * HD)
            q, k, v, d_heads = q_ref[here, lanes], k_ref[:, lanes], v_ref[:, lanes], heads_ref[here, lanes]
            delta = jnp.sum(d_heads.astype(F32) * attended_ref[here, lanes], axis=-1, keepdims=True)
            scores = matmul_last(q, k) * score_scale
            scores = jnp.where(hidden_keys, NEGATIVE, scores)
            probs = jnp.exp(scores - log_ref[here, head : head + 1])
            d_scores = (probs * (matmul_last(d_heads, v) - delta)).astype(BF16)
            dv_ref[:, lanes] += matmul_first(probs.astype(BF16), d_heads)
            dk_ref[:, lanes] += matmul_first(d_scores, q) * score_scale
            d_query = matmul(d_scores, k) * score_scale
            own_ref[7:8, lanes] += jnp.sum(d_query, axis=0, keepdims=True)
            stack[me, here, 2 * width + head * HD : 2 * width + (head + 1) * HD] = d_query.astype(BF16)
            turn = step * heads + head
            spread_steps(size, mine, output_ref, spread, turn * relays // turns, (turn + 1) * relays // turns)

    own_ref[7:8, width : 2 * width] = jnp.sum(dv_ref[...], axis=0, keepdims=True)
    stack[:, :, :width] = dk_ref[...].astype(BF16).reshape(sizes["ctx"], rows, width)
    stack[:, :, width : 2 * width] = dv_ref[...].astype(BF16).reshape(sizes["ctx"], rows, width)

    def span(step):
        flow, begin = step % 2, step // 2 * group
        return slice((flow * chunks + begin) * chunk, (flow * chunks + begin) * chunk + count)

    moving_keys = [
        [
            remote(
                stack.at[other, span(step), 0:wide],
                keys.at[me, span(step)],
                sem_keys[0].at[index, step],
                sem_keys[1].at[index, step],
                where,
            )
            for index, (other, where) in enumerate(others)
        ]
        for step in range(steps)
    ]
    for copies in moving_keys:
        for copy in copies:
            copy.start()
    small = send_all(lambda other: (own_ref, slots_v.at[rank]), peers, sem_small[0], sem_small[1])
    slots_v[rank] = own_ref[...]

    @pl.loop(0, model // 128)
    def _(index):
        columns = part_rows(index, 128)
        every = stack[...].reshape(total_keys, 3 * width)
        grads[columns, : 3 * width] = matmul_first(tokens[:, columns], every).astype(BF16)
        grads[columns, 3 * width :] = matmul_first(attn_low[:, columns], low_ref[...]).astype(BF16)

    near = near_start(data, grads, chip, sem_grads)
    state = {}

    def send_group(step):
        flow, begin = step % 2, step // 2 * group
        there = span(step)
        keys[me, there] = stack[me, there, 0:wide]
        for copy in moving_keys[step]:
            copy.wait_recv()
        total = keys[0, there].astype(F32)
        for index in range(1, sizes["ctx"]):
            total = total + keys[index, there].astype(F32)
        total_ref[there, 0:wide] = total.astype(BF16)
        total_ref[there, wide:] = stack[me, there, wide:]
        result = matmul_last(total_ref[there], flat[...]).astype(BF16)
        part[flow, begin : begin + group] = result.reshape(group, chunk, model)
        line_start_block(size, part, slots, line, flow, begin, group)

    def go_far():
        state["far"] = far_start(data, near, grads, chip, merged, far, sem_grads)
        wait_all(small)
        own = own_ref[...]
        row_ids = lax.broadcasted_iota(jnp.int32, own.shape, 0)
        grid_v[here_v] = jnp.where(row_ids < 6, slot_sum(slots_v, size), own)
        state["small"] = send_all(
            lambda other: (grid_v.at[here_v], grid_v.at[here_v]), everyone, sem_grid[0], sem_grid[1]
        )

    def go_across():
        wait_all(state["far"])
        value = slot_sum(far, data // 2).astype(BF16)
        state["across"] = blocks_start(sizes, value, blocks, sem_last)

    def finish(flow, k, total):
        return (total + d_attn[k]).astype(BF16)

    spread_steps(size, mine, output_ref, spread, relays, relays_sent)
    for step in range(2):
        send_group(step)
    between = [(1, go_far)]
    between += [(LAG + 2 * step - 3, functools.partial(send_group, step)) for step in range(2, steps)]
    between += [(max(LAG * size, LAG + 2 * steps), go_across)]
    line_run(size, part, slots, sums, full, line, finish, between)
    spread_steps(size, mine, output_ref, spread, relays_sent, relays_all)
    spread_end(size, mine, output_ref, spread)
    for copies in moving_keys:
        for copy in copies:
            copy.wait_send()
    wait_all(state["small"])
    vector_ref[...] = slot_sum(grid_v, data * sizes["ctx"])
    wait_all(moving_a)
    owned_a[...] = slot_sum(blocks_a, sizes["ctx"])
    wait_all(moving_b)
    owned_b[...] = slot_sum(blocks_b, sizes["ctx"])
    wait_all(state["across"])
    owned[...] = slot_sum(blocks, sizes["ctx"])


def unpack_kernel(
    full, output, owned, owned_a, owned_b, sums,
    output_ref, tokens_ref, qkv_ref, proj_ref, up_ref, down_ref, query_ref, value_ref, *rows
):
    width = qkv_ref.shape[2]
    output_ref[...] = output[...]
    tokens_ref[...] = full[...].astype(F32)
    for index, slot in enumerate((2, 0, 1)):
        qkv_ref[index] = owned[:, slot * width : (slot + 1) * width]
    proj_ref[...] = owned[:, 3 * width :].T
    up_ref[...] = owned_a[...]
    down_ref[...] = owned_b[...]
    query_ref[...] = sums[7, :width]
    value_ref[...] = sums[7, width : 2 * width]
    for index, row in enumerate(rows):
        row[...] = sums[index, : row.shape[0]]


def local_call(kernel, outs, scratch, args, name, scalars=1):
    return pl.pallas_call(
        kernel,
        out_shape=outs,
        in_specs=[pl.BlockSpec(memory_space=pltpu.SMEM)] * scalars + [VMEM_SPEC] * (len(args) - scalars),
        out_specs=[VMEM_SPEC] * len(outs),
        scratch_shapes=scratch,
        compiler_params=pltpu.CompilerParams(vmem_limit_bytes=60 * 2**20),
        name=name,
    )(*args)


def per_device(
    sizes,
    tokens,
    lengths,
    cotangent,
    qkv_weight,
    query_bias,
    value_bias,
    proj_weight,
    proj_bias,
    first_gain,
    first_shift,
    up_weight,
    up_bias,
    down_weight,
    down_bias,
    second_gain,
    second_shift,
):
    data, blocks, ranks = sizes["dp"], sizes["ctx"], sizes["tensor"]
    rows_in = tokens[0]
    row_count, model = rows_in.shape
    half = row_count // 2
    chunk = math.gcd(half, CHUNK)
    chunks = half // chunk
    piece, width = qkv_weight.shape[1:]
    up_width = up_weight.shape[1]
    keys = blocks * row_count
    score_scale = 1.0 / math.sqrt(HD)
    split = (2, chunks, chunk, model)
    flow = pltpu.VMEM(split, BF16)
    line = line_sems(chunks, 4)
    local = shaped(split[1:], F32)
    held = pltpu.VMEM(split[1:], F32)
    steps = 2 * chunks // math.gcd(chunks, GROUP)
    vector_width = max(model, up_width, 2 * width)
    given = (
        proj_bias, first_gain, first_shift, down_bias, second_gain, second_shift, up_bias, query_bias, value_bias
    )

    up_shape = (model, up_width)
    pair_slots = pltpu.VMEM((data // 2, model // data, up_width), BF16)
    pair_moves = sems(data // 2) + sems(max(1, data // 2 - 1))
    (
        queries, key_rows, value_rows, attended, attended_low, log_total, flat_proj, flat_qkv, wide_tokens,
        attn_low, d_attn, output_part, vectors, block_up, block_down,
    ) = call(
        functools.partial(front_kernel, sizes, score_scale, len(given)),
        [
            shaped((row_count, width), BF16),
            shaped((keys, width), BF16),
            shaped((keys, width), BF16),
            shaped((row_count, width), F32),
            shaped((row_count, width), BF16),
            shaped((row_count, width // HD), F32),
            shaped((width, model), BF16),
            shaped((model, 3 * width), BF16),
            shaped((blocks, row_count, model), BF16),
            shaped(split, BF16),
            local,
            shaped(split[1:], BF16),
            shaped((8, vector_width), F32),
            shaped((model // data, up_width), BF16),
            shaped((model // data, up_width), BF16),
        ],
        [
            pltpu.VMEM((3, model, width), BF16),
            pltpu.VMEM((data,) + proj_weight.shape, BF16),
            pltpu.VMEM((16, vector_width), F32),
            flow,
        ]
        + [
            pltpu.VMEM(up_shape, BF16),
            pltpu.VMEM(up_shape, BF16),
            flow,
            held,
            pltpu.VMEM((chunks, chunk, 1), F32),
            held,
            pltpu.VMEM((row_count, up_width), F32),
            pltpu.VMEM((row_count, up_width), BF16),
            flow,
            held,
            flow,
            pltpu.VMEM((row_count, up_width), BF16),
            flow,
            pltpu.VMEM(up_shape, BF16),
            pltpu.VMEM(up_shape, BF16),
        ]
        + [flow] * 6
        + [pair_slots] * 6
        + [DMA((max(1, blocks - 1), PIECES))] * 4
        + pair_sems(data) * 2
        + line * 3
        + pair_sems(data) * 2
        + pair_moves * 2,
        1,
        (lengths, rows_in, qkv_weight, proj_weight, cotangent[0].reshape(split), up_weight, down_weight.T) + given,
        "forward_and_hidden",
        scalars=1,
    )
    wide_tokens = wide_tokens.reshape(keys, model)

    own_shape = (model // data, 4 * width)
    last_pair = pltpu.VMEM((data // 2,) + own_shape, BF16)
    grad_tokens, output, own_last, own_up, own_down, sums = call(
        functools.partial(back_kernel, sizes, score_scale),
        [
            shaped(split, BF16),
            shaped(split, BF16),
            shaped(own_shape, F32),
            shaped((model // data, up_width), F32),
            shaped((model // data, up_width), F32),
            shaped(vectors.shape, F32),
        ],
        [
            pltpu.VMEM((keys, width), F32),
            pltpu.VMEM((keys, width), F32),
            pltpu.VMEM((row_count, width), BF16),
            pltpu.VMEM((blocks, row_count, 3 * width), BF16),
            pltpu.VMEM((model, 4 * width), BF16),
            pltpu.VMEM(vectors.shape, F32),
        ]
        + [flow] * 3
        + [
            pltpu.VMEM((blocks, row_count, 2 * width), BF16),
            pltpu.VMEM((row_count, 3 * width), BF16),
        ]
        + [last_pair] * 3
        + [pltpu.VMEM((blocks,) + own_shape, BF16)]
        + [pltpu.VMEM((blocks, model // data, up_width), BF16)] * 2
        + [
            pltpu.VMEM((ranks,) + vectors.shape, F32),
            pltpu.VMEM((data * blocks,) + vectors.shape, F32),
        ]
        + line
        + line_sems(chunks, 2)
        + [DMA((max(1, blocks - 1), steps))] * 2
        + pair_moves
        + sems(ranks - 1)
        + sems(data * blocks - 1)
        + sems(blocks - 1) * 3,
        2,
        (
            lengths, queries, key_rows, value_rows, attended, attended_low, log_total,
            flat_proj, attn_low.reshape(row_count, model), wide_tokens, vectors,
            flat_qkv, d_attn, block_up, block_down, output_part,
        ),
        "attention_backward",
        scalars=1,
    )
    output, grad_tokens, own_qkv, own_proj, own_up, own_down, grad_query, grad_value, *rows = local_call(
        unpack_kernel,
        [
            shaped((row_count, model), BF16),
            shaped((row_count, model), F32),
            shaped((3, model // data, width), F32),
            shaped((width, model // data), F32),
            shaped(own_up.shape, F32),
            shaped(own_down.shape, F32),
            shaped((width,), F32),
            shaped((width,), F32),
        ]
        + [shaped((model,), F32)] * 6
        + [shaped((up_width,), F32)],
        [],
        (
            grad_tokens.reshape(row_count, model),
            output.reshape(row_count, model),
            own_last,
            own_up,
            own_down,
            sums,
        ),
        "unpack",
        scalars=0,
    )
    return (
        output[None],
        grad_tokens[None],
        own_qkv,
        grad_query,
        grad_value,
        own_proj,
        rows[5],
        rows[4],
        rows[3],
        own_up,
        rows[6],
        own_down.T,
        rows[2],
        rows[1],
        rows[0],
    )


def solution(mesh):
    placed = (
        P("dp", "ctx", None),
        P("dp"),
        P("dp", "ctx", None),
        P(None, "dp", "tensor"),
        P("tensor"),
        P("tensor"),
        P("tensor", "dp"),
        P(),
        P(),
        P(),
        P("dp", "tensor"),
        P("tensor"),
        P("tensor", "dp"),
        P(),
        P(),
        P(),
    )
    return jax.shard_map(
        functools.partial(per_device, dict(mesh.shape)),
        mesh=mesh,
        in_specs=placed,
        out_specs=(
            P("dp", "ctx", None),
            P("dp", "ctx", None),
            P(None, "dp", "tensor"),
            P("tensor"),
            P("tensor"),
            P("tensor", "dp"),
            P(),
            P(),
            P(),
            P("dp", "tensor"),
            P("tensor"),
            P("tensor", "dp"),
            P(),
            P(),
            P(),
        ),
        check_vma=False,
    )
```
